128 devices in a mesh: front: 4 (over x_lo, core), row: 8 (over x_hi, y), col: 4 (over z).
Axes of the slice: x: 4 (x_hi: 2, x_lo: 2; x = x_hi * 2 + x_lo), y: 4, z: 4, core: 2. Of those that a mesh axis runs over, the one named last changes fastest.
Arguments:
- parent_entries: float32 [12288, 12288], P('row', ('front', 'col')), as said below
- child_update: float32 [4, 8192, 8192], P('front', 'row', 'col'), as said below
- child_map: int32 [4, 64], replicated, may hold values from 0 to 95, as said below
- child_mask: int32 [4, 64, 64], P('front'), may hold values from 0 to 1, as said below
Outputs:
- schur: float32 [12288, 12288], P('row', ('front', 'col'))
- panel: float32 [12288, 512], P('row')
The draws below stay inside these ranges and needn't reach their ends.
Inputs may be any that keep to these rules, and one draw needn't show every extreme that they name: `child_update`: each child's update matrix is symmetric. `parent_entries`: Symmetric. `child_mask`: symmetric in its last two dimensions, ones on the diagonal. Distinct within each child. With v = j mod (16), e = v mod (1), r = (v mod 8) div (1), k = (v div 8) * 1 + e and g = r * 2 + k div (1), child_map[f, j] div (6) equals g.
All inputs are finite; a program needn't handle non-finite values.
Results may differ from the reference program's by a relative error of at most 0.000071.
Values sent between devices are 32-bit elements; how exact they have to be, the bound alone decides.
No kernel may reach another device: no remote copies, remote signals or barrier semaphores. Data moves between devices by JAX's collectives and lax.ppermute only.
A program may use at most 128 MiB of HBM per device.

```python
import math
import jax
import jax.numpy as jnp
from jax import lax

NP = 12288
MC = 8192
W = 512
BLK = 128
GRID_ROWS = 8
GRID_COLS = 4
GROUPS = 16
FRONTS = 4
MB = 64
PB = 96
SPAN = 8


def draw_parent_entries(key, part):
    noise = jax.random.normal(key, (NP, NP), jnp.float32)
    diagonal = jax.random.uniform(jax.random.fold_in(key, 1), (NP,), jnp.float32, 6.0, 9.0)
    mirrored = (noise + noise.T) * 0.70710678
    lines = jnp.arange(NP)
    leading = lines < W
    both_leading = leading[:, None] & leading[None, :]
    one_leading = leading[:, None] != leading[None, :]
    spread = jnp.where(both_leading, 0.8 / math.sqrt(W), jnp.where(one_leading, 2.2 / math.sqrt(NP), 0.5 / math.sqrt(NP)))
    onto = lines[:, None] == lines[None, :]
    return mirrored * spread + jnp.where(onto, diagonal[:, None], 0.0)


def draw_child_update(key, part):
    noise = jax.random.normal(key, (FRONTS, MC, MC), jnp.float32)
    mirrored = (noise + jnp.swapaxes(noise, 1, 2)) * (0.70710678 / math.sqrt(MC))
    return mirrored


def draw_child_mask(key, part):
    values = jax.random.randint(key, (FRONTS, MB, MB), 0, 5)
    keep = jnp.where(values < 3, 1, 0).astype(jnp.int32)
    lines = jnp.arange(MB)
    upper = lines[:, None] <= lines[None, :]
    mirrored = jnp.where(upper[None], keep, jnp.swapaxes(keep, 1, 2))
    onto = lines[:, None] == lines[None, :]
    return jnp.where(onto[None], 1, mirrored).astype(jnp.int32)


def draw_child_map(key, part):
    blocks = jnp.arange(MB, dtype=jnp.int32)
    column_blocks = MB // GRID_COLS
    share = SPAN // GRID_ROWS
    within = blocks % column_blocks
    row_part = within % SPAN // share
    rank_part = within // SPAN * share + within % SPAN % share
    target = row_part * (GROUPS // GRID_ROWS) + rank_part // (column_blocks // GROUPS)
    earlier = (target[:, None] == target[None, :]) & (blocks[None, :] < blocks[:, None])
    order = jnp.sum(earlier.astype(jnp.int32), axis=1)
    slots = PB // GROUPS
    scores = jax.random.randint(key, (FRONTS, GROUPS, slots), 0, 1 << 20) * slots + jnp.arange(slots, dtype=jnp.int32)
    shuffled = jnp.argsort(scores, axis=-1).astype(jnp.int32)
    chosen = shuffled[:, target, order]
    return (target[None, :] * slots + chosen).astype(jnp.int32)


def setup_inputs(seed: int = 0) -> dict:
    streams_of = jax.random.split(jax.random.key(seed), 5)
    parent_entries = draw_parent_entries(jax.random.fold_in(streams_of[4], 71), 0)
    child_update = draw_child_update(jax.random.fold_in(streams_of[4], 71), 0)
    child_map = draw_child_map(jax.random.fold_in(streams_of[4], 71), 0)
    child_mask = draw_child_mask(jax.random.fold_in(streams_of[4], 71), 0)
    return dict(parent_entries=parent_entries, child_update=child_update, child_map=child_map, child_mask=child_mask)


def reference(parent_entries, child_update, child_map, child_mask):
    front = parent_entries
    offsets = jnp.arange(BLK, dtype=jnp.int32)
    for child in range(FRONTS):
        spread = jnp.repeat(jnp.repeat(child_mask[child], BLK, axis=0), BLK, axis=1)
        masked = child_update[child] * spread.astype(child_update.dtype)
        places = (child_map[child][:, None] * BLK + offsets[None, :]).reshape(-1).astype(jnp.int32)
        front = front.at[places[:, None], places[None, :]].add(masked)
    factor = jnp.linalg.cholesky(front[:W, :W])
    panel = jax.scipy.linalg.solve_triangular(factor, front[:, :W].T, lower=True).T
    schur = front - jnp.dot(panel, panel.T, precision=lax.Precision.HIGHEST)
    lines = jnp.arange(NP)
    keep = (lines[:, None] >= W) & (lines[None, :] >= W)
    schur = jnp.where(keep, schur, jnp.zeros_like(schur))
    return (schur, panel)
```

```python
import functools

import jax
import jax.numpy as jnp
from jax import lax
from jax.experimental import pallas as pl
from jax.experimental.pallas import tpu as pltpu
from jax.sharding import PartitionSpec as P

W = 512
BLK = 128
FRONTS = 4
ROWS = 8
COLS = 4
GROUPS = 16
PR = 12
PC = 6
WB = W // BLK
ALL = ("front", "row", "col")
GRP = ("front", "col")
HIGHEST = lax.Precision.HIGHEST


def group_column(group):
    return group // 2 + 8 * (group % 2)


def pack_kernel(mask_ref, x_ref, o_ref):
    step = pl.program_id(0)
    for front in range(FRONTS):
        for col in range(COLS):
            v = group_column(front * COLS + col)
            keep = mask_ref[step, v].astype(jnp.float32)
            o_ref[front, 0, col] = x_ref[:, v * BLK : (v + 1) * BLK] * keep


def pack(window, local):
    return pl.pallas_call(
        pack_kernel,
        name="pack",
        grid_spec=pltpu.PrefetchScalarGridSpec(
            num_scalar_prefetch=1,
            grid=(ROWS,),
            in_specs=[pl.BlockSpec((BLK, GROUPS * BLK), lambda i, m: (i, 0))],
            out_specs=pl.BlockSpec(
                (FRONTS, 1, COLS, BLK, BLK), lambda i, m: (0, i, 0, 0, 0)
            ),
        ),
        out_shape=jax.ShapeDtypeStruct((FRONTS, ROWS, COLS, BLK, BLK), jnp.float32),
        compiler_params=pltpu.CompilerParams(vmem_limit_bytes=32 << 20),
    )(window, local)


def slice_kernel(inv_row_ref, inv_lead_ref, recv_ref, parent_ref, o_ref):
    for a in range(PR):
        for q in range(WB):
            total = parent_ref[a, :, q * BLK : (q + 1) * BLK]
            for front in range(FRONTS):
                r = inv_row_ref[front, a]
                c = inv_lead_ref[front, q]
                ok = jnp.logical_and(r >= 0, c >= 0).astype(jnp.float32)
                source = front * 32 + jnp.maximum(r, 0) * COLS + jnp.maximum(c, 0)
                total = total + recv_ref[source] * ok
            o_ref[a, :, q * BLK : (q + 1) * BLK] = total


def assemble_slices(inv_row, inv_lead, recv, parent):
    smem = pl.BlockSpec(memory_space=pltpu.SMEM)
    vmem = pl.BlockSpec(memory_space=pltpu.VMEM)
    return pl.pallas_call(
        slice_kernel,
        name="slices",
        in_specs=[smem, smem, vmem, vmem],
        out_specs=vmem,
        out_shape=jax.ShapeDtypeStruct((PR, 8, W), jnp.float32),
    )(inv_row, inv_lead, recv, parent)


def final_kernel(inv_row_ref, inv_col_ref, lead_ref, *refs):
    recvs = refs[:FRONTS]
    parent_ref, panel_ref, across_ref, o_ref = refs[FRONTS:]
    a = pl.program_id(0)
    product = lax.dot_general(
        panel_ref[...],
        across_ref[...],
        (((1,), (1,)), ((), ())),
        precision=HIGHEST,
        preferred_element_type=jnp.float32,
    )
    o_ref[...] = parent_ref[...] - product
    for b in range(PC):
        span = slice(b * BLK, (b + 1) * BLK)
        total = o_ref[:, span]
        for front in range(FRONTS):
            r = inv_row_ref[front, a]
            c = inv_col_ref[front, b]
            ok = jnp.logical_and(r >= 0, c >= 0).astype(jnp.float32)
            total = total + recvs[front][jnp.maximum(c, 0)] * ok
        o_ref[:, span] = total
    leading_row = jnp.logical_and(lead_ref[0] == 1, a < WB)

    @pl.when(leading_row)
    def _():
        o_ref[...] = jnp.zeros_like(o_ref)

    @pl.when(lead_ref[1] == 1)
    def _():
        o_ref[:, :W] = jnp.zeros((BLK, W), jnp.float32)


def finish(inv_row, inv_col, lead, recv, parent, panel, across):
    def recv_map(front):
        return lambda a, ir, ic, ld: (front * ROWS + jnp.maximum(ir[front, a], 0), 0, 0)

    return pl.pallas_call(
        final_kernel,
        name="finish",
        grid_spec=pltpu.PrefetchScalarGridSpec(
            num_scalar_prefetch=3,
            grid=(PR,),
            in_specs=[
                pl.BlockSpec((COLS, BLK, BLK), recv_map(front)) for front in range(FRONTS)
            ]
            + [
                pl.BlockSpec((BLK, PC * BLK), lambda a, *_: (a, 0)),
                pl.BlockSpec((BLK, W), lambda a, *_: (a, 0)),
                pl.BlockSpec((PC * BLK, W), lambda a, *_: (0, 0)),
            ],
            out_specs=pl.BlockSpec((BLK, PC * BLK), lambda a, *_: (a, 0)),
        ),
        out_shape=jax.ShapeDtypeStruct((PR * BLK, PC * BLK), jnp.float32),
        compiler_params=pltpu.CompilerParams(vmem_limit_bytes=40 << 20),
    )(inv_row, inv_col, lead, recv, recv, recv, recv, parent, panel, across)


def inverse_places(places, length):
    count = places.shape[1]
    hits = places[:, :, None] == jnp.arange(length, dtype=jnp.int32)
    order = jnp.arange(1, count + 1, dtype=jnp.int32)[None, :, None]
    return jnp.sum(jnp.where(hits, order, 0), axis=1) - 1


def scatter_from_first(x, axis, parts):
    index = lax.axis_index(axis)
    total = jnp.where(index == 0, parts(x, 0), 0.0)
    for k in range(1, lax.axis_size(axis)):
        total = total + lax.ppermute(parts(x, k), axis, [(0, k)])
    return total


def swap_pairs(flip):
    pairs = []
    for front in range(FRONTS):
        for row in range(ROWS):
            for col in range(COLS):
                group = front * COLS + col
                half = group % 2 if flip == 0 else 1 - group % 2
                to_row, to_group = group // 2, 2 * row + half
                target = (to_group // COLS) * 32 + to_row * COLS + to_group % COLS
                pairs.append((front * 32 + row * COLS + col, target))
    return pairs


def body(parent_entries, child_update, child_map, child_mask):
    row = lax.axis_index("row")
    front = lax.axis_index("front")
    col = lax.axis_index("col")
    group = front * COLS + col
    local = child_update[0]
    window = lax.dynamic_slice(child_mask[0], (row * ROWS, col * GROUPS), (ROWS, GROUPS))

    lead_keep = window[:, 0].astype(jnp.float32)
    lead = local[:, :BLK].reshape(ROWS, FRONTS, COLS, 8, BLK) * lead_keep[:, None, None, None, None]
    lead = lead.transpose(1, 0, 2, 3, 4).reshape(128, 8, BLK)
    lead_recv = lax.all_to_all(lead, ALL, 0, 0, tiled=True)

    first = parent_entries[:, :W].reshape(PR, FRONTS, COLS, 8, W)
    first = scatter_from_first(first, "col", lambda x, k: x[:, :, k])
    first = scatter_from_first(first, "front", lambda x, k: x[:, k])

    column = group // 2 + 8 * (group % 2)
    by_row = lax.dynamic_index_in_dim(child_map.reshape(FRONTS, ROWS, 8), row, 2, keepdims=False)
    by_col = lax.dynamic_index_in_dim(
        child_map.reshape(FRONTS, COLS, GROUPS), column, 2, keepdims=False
    )
    inv_row = inverse_places(by_row - row * PR, PR)
    inv_col = inverse_places(by_col - group * PC, PC)
    inv_lead = inverse_places(child_map.reshape(FRONTS, COLS, GROUPS)[:, :, 0], WB)

    slices = assemble_slices(inv_row, inv_lead, lead_recv, first)

    corner = jnp.broadcast_to(slices[:WB].reshape(1, WB * 8, W), (ROWS, WB * 8, W))
    corner = lax.all_to_all(corner, "row", 0, 0, tiled=True)[0]
    corner = jnp.broadcast_to(corner[None], (GROUPS, WB * 8, W))
    corner = lax.all_to_all(corner, GRP, 0, 0, tiled=True)
    corner = corner.reshape(GROUPS, WB, 8, W).transpose(1, 0, 2, 3).reshape(W, W)

    packed = pack(window, local).reshape(128, BLK, BLK)
    recv = lax.all_to_all(packed, ALL, 0, 0, tiled=True)

    rows_raw = lax.all_gather(slices.reshape(PR * 8, W), GRP, axis=0, tiled=True)
    rows_raw = rows_raw.reshape(GROUPS, PR, 8, W).transpose(1, 0, 2, 3).reshape(PR * BLK, W)

    even = group % 2 == 0
    one = lax.ppermute(jnp.where(even, slices[:PC], slices[PC:]), ALL, swap_pairs(0))
    two = lax.ppermute(jnp.where(even, slices[PC:], slices[:PC]), ALL, swap_pairs(1))
    mine = jnp.stack([jnp.where(even, one, two), jnp.where(even, two, one)], axis=1)
    cols_raw = lax.all_gather(mine.reshape(PC * 16, W), "row", axis=0, tiled=True)
    cols_raw = cols_raw.reshape(ROWS, PC, 16, W).transpose(1, 0, 2, 3).reshape(PC * BLK, W)

    factor = jnp.linalg.cholesky(corner)
    inverse = jax.scipy.linalg.solve_triangular(factor, jnp.eye(W, dtype=jnp.float32), lower=True)
    panel = jnp.dot(rows_raw, inverse.T, precision=HIGHEST)
    across = jnp.dot(cols_raw, inverse.T, precision=HIGHEST)
    lead_flags = jnp.stack([row == 0, group == 0]).astype(jnp.int32)
    schur = finish(inv_row, inv_col, lead_flags, recv, parent_entries, panel, across)
    return schur, panel


def solution(mesh):
    placed = (P("row", ("front", "col")), P("front", "row", "col"), P(), P("front", None, None))
    return jax.shard_map(
        body,
        mesh=mesh,
        in_specs=placed,
        out_specs=(P("row", ("front", "col")), P("row", None)),
        check_vma=False,
    )
```

```python
import functools

import jax
import jax.numpy as jnp
from jax import lax
from jax.experimental import pallas as pl
from jax.experimental.pallas import tpu as pltpu
from jax.sharding import PartitionSpec as P

W = 512
BLK = 128
FRONTS = 4
ROWS = 8
COLS = 4
GROUPS = 16
PR = 12
PC = 6
WB = W // BLK
ALL = ("front", "row", "col")
GRP = ("front", "col")
HIGHEST = lax.Precision.HIGHEST


def group_column(group):
    return group // 2 + 8 * (group % 2)


def pack_kernel(mask_ref, x_ref, o_ref):
    step = pl.program_id(0)
    for front in range(FRONTS):
        for col in range(COLS):
            v = group_column(front * COLS + col)
            keep = mask_ref[step, v].astype(jnp.float32)
            o_ref[front, 0, col] = x_ref[:, v * BLK : (v + 1) * BLK] * keep


def pack(window, local):
    return pl.pallas_call(
        pack_kernel,
        name="pack",
        grid_spec=pltpu.PrefetchScalarGridSpec(
            num_scalar_prefetch=1,
            grid=(ROWS,),
            in_specs=[pl.BlockSpec((BLK, GROUPS * BLK), lambda i, m: (i, 0))],
            out_specs=pl.BlockSpec(
                (FRONTS, 1, COLS, BLK, BLK), lambda i, m: (0, i, 0, 0, 0)
            ),
        ),
        out_shape=jax.ShapeDtypeStruct((FRONTS, ROWS, COLS, BLK, BLK), jnp.float32),
        compiler_params=pltpu.CompilerParams(vmem_limit_bytes=32 << 20),
    )(window, local)


def slice_kernel(inv_row_ref, inv_lead_ref, recv_ref, parent_ref, o_ref):
    for a in range(PR):
        for q in range(WB):
            total = parent_ref[a, :, q * BLK : (q + 1) * BLK]
            for front in range(FRONTS):
                r = inv_row_ref[front, a]
                c = inv_lead_ref[front, q]
                ok = jnp.logical_and(r >= 0, c >= 0).astype(jnp.float32)
                source = front * 32 + jnp.maximum(r, 0) * COLS + jnp.maximum(c, 0)
                total = total + recv_ref[source] * ok
            o_ref[a, :, q * BLK : (q + 1) * BLK] = total


def assemble_slices(inv_row, inv_lead, recv, parent):
    smem = pl.BlockSpec(memory_space=pltpu.SMEM)
    vmem = pl.BlockSpec(memory_space=pltpu.VMEM)
    return pl.pallas_call(
        slice_kernel,
        name="slices",
        in_specs=[smem, smem, vmem, vmem],
        out_specs=vmem,
        out_shape=jax.ShapeDtypeStruct((PR, 8, W), jnp.float32),
    )(inv_row, inv_lead, recv, parent)


KB = 4


def factor_diagonal(get, put):
    groups = BLK // 8
    a = [get(g) for g in range(groups)]
    lanes = lax.broadcasted_iota(jnp.int32, (8, BLK), 1)
    subs = lax.broadcasted_iota(jnp.int32, (8, BLK), 0)
    e = [jnp.where(lanes == subs + 8 * g, 1.0, 0.0).astype(jnp.float32) for g in range(groups)]
    full = (8, BLK)
    for j0 in range(0, BLK, KB):
        g0, i0 = j0 // 8, j0 % 8
        head = [jnp.broadcast_to(a[g0][:, j0 + k : j0 + k + 1], full) for k in range(KB)]
        small = [[None] * KB for _ in range(KB)]
        for i in range(KB):
            for k in range(i + 1):
                small[i][k] = jnp.broadcast_to(head[k][i0 + i : i0 + i + 1, :], full)
        inv = [None] * KB
        low = [[None] * KB for _ in range(KB)]
        for k in range(KB):
            root = lax.rsqrt(small[k][k])
            inv[k] = root * (1.5 - 0.5 * small[k][k] * root * root)
            for i in range(k + 1, KB):
                low[i][k] = small[i][k] * inv[k]
            for i in range(k + 1, KB):
                for m in range(k + 1, i + 1):
                    small[i][m] = small[i][m] - low[i][k] * low[m][k]
        u, w = [], []
        for k in range(KB):
            r = jnp.broadcast_to(a[g0][i0 + k : i0 + k + 1, :], full)
            s = jnp.broadcast_to(e[g0][i0 + k : i0 + k + 1, :], full)
            for m in range(k):
                r = r - low[k][m] * u[m]
                s = s - low[k][m] * w[m]
            u.append(r * inv[k])
            w.append(s * inv[k])
        for g in range(g0, groups):
            if g == g0 and i0 + KB == 8:
                pass
            else:
                mult = []
                for k in range(KB):
                    c = head[k] if g == g0 else jnp.broadcast_to(a[g][:, j0 + k : j0 + k + 1], full)
                    for m in range(k):
                        c = c - mult[m] * low[k][m]
                    mult.append(c * inv[k])
                if g == g0:
                    mult = [jnp.where(subs >= i0 + KB, c, 0.0) for c in mult]
                for k in range(KB):
                    a[g] = a[g] - mult[k] * u[k]
                    e[g] = e[g] - mult[k] * w[k]
            if g == g0:
                for k in range(KB):
                    e[g] = jnp.where(subs == i0 + k, w[k], e[g])
        if i0 + KB == 8:
            put(g0, e[g0])


def factor_kernel(place_ref, *refs):
    pieces = refs[:COLS]
    w_ref, m_ref, d_ref = refs[COLS:]
    for other in range(COLS):
        for slot in range(FRONTS):
            source = place_ref[1] ^ (slot * COLS + other)
            for block in range(WB):
                start = pl.multiple_of(block * BLK + source * 8, 8)
                m_ref[pl.ds(start, 8), :W] = pieces[other][slot, block]
    lanes = lax.broadcasted_iota(jnp.int32, (BLK, BLK), 1)
    subs = lax.broadcasted_iota(jnp.int32, (BLK, BLK), 0)
    eye = jnp.where(lanes == subs, 1.0, 0.0).astype(jnp.float32)
    m_ref[:, W:] = jnp.zeros((W, W), jnp.float32)
    for block in range(W // BLK):
        m_ref[block * BLK : (block + 1) * BLK, W + block * BLK : W + (block + 1) * BLK] = eye

    def step(block, carry):
        base = pl.multiple_of(block * BLK, BLK)

        def get(g):
            return m_ref[pl.ds(pl.multiple_of(base + g * 8, 8), 8), pl.ds(base, BLK)]

        def put(g, value):
            d_ref[g * 8 : (g + 1) * 8, :] = value

        factor_diagonal(get, put)
        rows = jnp.dot(
            d_ref[...], m_ref[pl.ds(base, BLK), :], precision=HIGHEST, preferred_element_type=jnp.float32
        )
        m_ref[pl.ds(base, BLK), :] = rows

        @pl.when(block < W // BLK - 1)
        def _():
            column = lax.broadcasted_iota(jnp.int32, (BLK, W), 1)
            later = jnp.where(column >= base + BLK, rows[:, :W], 0.0)
            m_ref[...] = m_ref[...] - lax.dot_general(
                later, rows, (((0,), (0,)), ((), ())), precision=HIGHEST, preferred_element_type=jnp.float32
            )

        return carry

    lax.fori_loop(0, W // BLK, step, 0)
    w_ref[...] = m_ref[:, W:]


def factor_inverse(place, pieces):
    vmem = pl.BlockSpec(memory_space=pltpu.VMEM)
    return pl.pallas_call(
        factor_kernel,
        name="factor",
        in_specs=[pl.BlockSpec(memory_space=pltpu.SMEM)] + [vmem] * COLS,
        out_specs=vmem,
        out_shape=jax.ShapeDtypeStruct((W, W), jnp.float32),
        scratch_shapes=[pltpu.VMEM((W, 2 * W), jnp.float32), pltpu.VMEM((BLK, BLK), jnp.float32)],
        compiler_params=pltpu.CompilerParams(vmem_limit_bytes=40 << 20),
    )(place, *pieces)


def panel_kernel(place_ref, rows_ref, *refs):
    cols = refs[:4]
    inverse_ref, panel_ref, high_ref, low_ref, block_ref = refs[4:]
    step = pl.program_id(0)

    def times_inverse(x):
        return lax.dot_general(
            x,
            inverse_ref[...],
            (((1,), (1,)), ((), ())),
            precision=HIGHEST,
            preferred_element_type=jnp.float32,
        )

    @pl.when(step < PR)
    def _():
        panel_ref[...] = times_inverse(rows_ref[:, 0].reshape(BLK, W))

    @pl.when(step >= PR)
    def _():
        for other in range(4):
            for slot in range(2):
                source = place_ref[0] ^ (slot * 4 + other)
                start = pl.multiple_of(source * 16, 16)
                block_ref[pl.ds(start, 16), :] = cols[other][slot, 0]
        value = times_inverse(block_ref[...])
        high = value.astype(jnp.bfloat16)
        high_ref[...] = high
        low_ref[...] = (value - high.astype(jnp.float32)).astype(jnp.bfloat16)


def make_panels(place, rows_raw, cols_raw, inverse):
    def in_rows(i):
        return jnp.minimum(i, PR - 1)

    def in_cols(i):
        return jnp.maximum(i - PR, 0)

    half = jax.ShapeDtypeStruct((PC * BLK, W), jnp.bfloat16)
    return pl.pallas_call(
        panel_kernel,
        name="panels",
        grid_spec=pltpu.PrefetchScalarGridSpec(
            num_scalar_prefetch=1,
            grid=(PR + PC,),
            in_specs=[pl.BlockSpec((GROUPS, 1, 8, W), lambda i, p: (0, in_rows(i), 0, 0))]
            + [pl.BlockSpec((2, 1, 16, W), lambda i, p: (0, in_cols(i), 0, 0))] * 4
            + [pl.BlockSpec((W, W), lambda i, p: (0, 0))],
            out_specs=[
                pl.BlockSpec((BLK, W), lambda i, p: (in_rows(i), 0)),
                pl.BlockSpec((BLK, W), lambda i, p: (in_cols(i), 0)),
                pl.BlockSpec((BLK, W), lambda i, p: (in_cols(i), 0)),
            ],
            scratch_shapes=[pltpu.VMEM((BLK, W), jnp.float32)],
        ),
        out_shape=[jax.ShapeDtypeStruct((PR * BLK, W), jnp.float32), half, half],
        compiler_params=pltpu.CompilerParams(vmem_limit_bytes=32 << 20),
    )(place, rows_raw, *cols_raw, inverse)


def final_kernel(inv_row_ref, inv_col_ref, lead_ref, *refs):
    recvs = refs[:FRONTS]
    parent_ref, panel_ref, high_ref, low_ref, o_ref = refs[FRONTS:]
    a = pl.program_id(0)
    panel = panel_ref[...]
    panel_high = panel.astype(jnp.bfloat16)
    panel_low = (panel - panel_high.astype(jnp.float32)).astype(jnp.bfloat16)

    def product(x, y):
        return lax.dot_general(
            x, y, (((1,), (1,)), ((), ())), preferred_element_type=jnp.float32
        )

    total = product(panel_high, low_ref[...]) + product(panel_low, high_ref[...])
    o_ref[...] = parent_ref[...] - (total + product(panel_high, high_ref[...]))
    for b in range(PC):
        span = slice(b * BLK, (b + 1) * BLK)
        total = o_ref[:, span]
        for front in range(FRONTS):
            r = inv_row_ref[front, a]
            c = inv_col_ref[front, b]
            ok = jnp.logical_and(r >= 0, c >= 0).astype(jnp.float32)
            total = total + recvs[front][jnp.maximum(c, 0)] * ok
        o_ref[:, span] = total
    leading_row = jnp.logical_and(lead_ref[0] == 1, a < WB)

    @pl.when(leading_row)
    def _():
        o_ref[...] = jnp.zeros_like(o_ref)

    @pl.when(lead_ref[1] == 1)
    def _():
        o_ref[:, :W] = jnp.zeros((BLK, W), jnp.float32)


def finish(inv_row, inv_col, lead, recv, parent, panel, high, low):
    def recv_map(front):
        return lambda a, ir, ic, ld: (front * ROWS + jnp.maximum(ir[front, a], 0), 0, 0)

    whole = pl.BlockSpec((PC * BLK, W), lambda a, *_: (0, 0))
    return pl.pallas_call(
        final_kernel,
        name="finish",
        grid_spec=pltpu.PrefetchScalarGridSpec(
            num_scalar_prefetch=3,
            grid=(PR,),
            in_specs=[
                pl.BlockSpec((COLS, BLK, BLK), recv_map(front)) for front in range(FRONTS)
            ]
            + [
                pl.BlockSpec((BLK, PC * BLK), lambda a, *_: (a, 0)),
                pl.BlockSpec((BLK, W), lambda a, *_: (a, 0)),
                whole,
                whole,
            ],
            out_specs=pl.BlockSpec((BLK, PC * BLK), lambda a, *_: (a, 0)),
        ),
        out_shape=jax.ShapeDtypeStruct((PR * BLK, PC * BLK), jnp.float32),
        compiler_params=pltpu.CompilerParams(vmem_limit_bytes=40 << 20),
    )(inv_row, inv_col, lead, recv, recv, recv, recv, parent, panel, high, low)


def inverse_places(places, length):
    count = places.shape[1]
    hits = places[:, :, None] == jnp.arange(length, dtype=jnp.int32)
    order = jnp.arange(1, count + 1, dtype=jnp.int32)[None, :, None]
    return jnp.sum(jnp.where(hits, order, 0), axis=1) - 1


def scatter_from_first(x, axis, parts):
    index = lax.axis_index(axis)
    total = jnp.where(index == 0, parts(x, 0), 0.0)
    for k in range(1, lax.axis_size(axis)):
        total = total + lax.ppermute(parts(x, k), axis, [(0, k)])
    return total


def flipped(x, axis, bits):
    size = lax.axis_size(axis)
    return lax.ppermute(x, axis, [(i, i ^ bits) for i in range(size)])


def swap_pairs(flip):
    pairs = []
    for front in range(FRONTS):
        for row in range(ROWS):
            for col in range(COLS):
                group = front * COLS + col
                half = group % 2 if flip == 0 else 1 - group % 2
                to_row, to_group = group // 2, 2 * row + half
                target = (to_group // COLS) * 32 + to_row * COLS + to_group % COLS
                pairs.append((front * 32 + row * COLS + col, target))
    return pairs


def body(parent_entries, child_update, child_map, child_mask):
    row = lax.axis_index("row")
    front = lax.axis_index("front")
    col = lax.axis_index("col")
    group = front * COLS + col
    local = child_update[0]
    window = lax.dynamic_slice(child_mask[0], (row * ROWS, col * GROUPS), (ROWS, GROUPS))

    lead_keep = window[:, 0].astype(jnp.float32)
    lead = local[:, :BLK].reshape(ROWS, FRONTS, COLS, 8, BLK) * lead_keep[:, None, None, None, None]
    lead = lead.transpose(1, 0, 2, 3, 4).reshape(128, 8, BLK)
    lead_recv = lax.all_to_all(lead, ALL, 0, 0, tiled=True)

    first = parent_entries[:, :W].reshape(PR, FRONTS, COLS, 8, W)
    first = scatter_from_first(first, "col", lambda x, k: x[:, :, k])
    first = scatter_from_first(first, "front", lambda x, k: x[:, k])

    column = group // 2 + 8 * (group % 2)
    by_row = lax.dynamic_index_in_dim(child_map.reshape(FRONTS, ROWS, 8), row, 2, keepdims=False)
    by_col = lax.dynamic_index_in_dim(
        child_map.reshape(FRONTS, COLS, GROUPS), column, 2, keepdims=False
    )
    inv_row = inverse_places(by_row - row * PR, PR)
    inv_col = inverse_places(by_col - group * PC, PC)
    inv_lead = inverse_places(child_map.reshape(FRONTS, COLS, GROUPS)[:, :, 0], WB)

    slices = assemble_slices(inv_row, inv_lead, lead_recv, first)

    corner = slices[:WB]
    near = jnp.where(row == 0, corner, 0.0)
    for k in range(1, 4):
        near = near + lax.ppermute(corner, "row", [(0, k)])
    far = lax.ppermute(near, "row", [(k, 4 + k) for k in range(4)])
    corner = jnp.where(row < 4, near, far)
    corner = jnp.stack([corner, flipped(corner, "front", 1)])
    corner = jnp.concatenate([corner, flipped(corner, "front", 2)])
    pieces = [corner] + [flipped(corner, "col", bits) for bits in range(1, COLS)]
    place = jnp.stack([row, group]).astype(jnp.int32)
    inverse = factor_inverse(place, pieces)

    packed = pack(window, local).reshape(128, BLK, BLK)
    recv = lax.all_to_all(packed, ALL, 0, 0, tiled=True)

    rows_raw = lax.all_gather(slices.reshape(PR * 8, W), GRP, axis=0, tiled=True)
    rows_raw = rows_raw.reshape(GROUPS, PR, 8, W)

    even = group % 2 == 0
    one = lax.ppermute(jnp.where(even, slices[:PC], slices[PC:]), ALL, swap_pairs(0))
    two = lax.ppermute(jnp.where(even, slices[PC:], slices[:PC]), ALL, swap_pairs(1))
    mine = jnp.stack([jnp.where(even, one, two), jnp.where(even, two, one)], axis=1)
    mine = mine.reshape(PC, 16, W)
    mine = jnp.stack([mine, flipped(mine, "row", 4)])
    cols_raw = [mine] + [flipped(mine, "row", bits) for bits in range(1, 4)]

    panel, high, low = make_panels(place, rows_raw, cols_raw, inverse)
    lead_flags = jnp.stack([row == 0, group == 0]).astype(jnp.int32)
    schur = finish(inv_row, inv_col, lead_flags, recv, parent_entries, panel, high, low)
    return schur, panel


def solution(mesh):
    placed = (P("row", ("front", "col")), P("front", "row", "col"), P(), P("front", None, None))
    return jax.shard_map(
        body,
        mesh=mesh,
        in_specs=placed,
        out_specs=(P("row", ("front", "col")), P("row", None)),
        check_vma=False,
    )
```

```python
import functools

import jax
import jax.numpy as jnp
from jax import lax
from jax.experimental import pallas as pl
from jax.experimental.pallas import tpu as pltpu
from jax.sharding import PartitionSpec as P

W = 512
BLK = 128
FRONTS = 4
ROWS = 8
COLS = 4
GROUPS = 16
PR = 12
PC = 6
WB = W // BLK
ALL = ("front", "row", "col")
GRP = ("front", "col")
HIGHEST = lax.Precision.HIGHEST


def group_column(group):
    return group // 2 + 8 * (group % 2)


def pack_kernel(mask_ref, x_ref, o_ref):
    step = pl.program_id(0)
    for front in range(FRONTS):
        for col in range(COLS):
            v = group_column(front * COLS + col)
            keep = mask_ref[step, v].astype(jnp.float32)
            o_ref[front, 0, col] = x_ref[:, v * BLK : (v + 1) * BLK] * keep


def pack(window, local):
    return pl.pallas_call(
        pack_kernel,
        name="pack",
        grid_spec=pltpu.PrefetchScalarGridSpec(
            num_scalar_prefetch=1,
            grid=(ROWS,),
            in_specs=[pl.BlockSpec((BLK, GROUPS * BLK), lambda i, m: (i, 0))],
            out_specs=pl.BlockSpec(
                (FRONTS, 1, COLS, BLK, BLK), lambda i, m: (0, i, 0, 0, 0)
            ),
        ),
        out_shape=jax.ShapeDtypeStruct((FRONTS, ROWS, COLS, BLK, BLK), jnp.float32),
        compiler_params=pltpu.CompilerParams(vmem_limit_bytes=32 << 20),
    )(window, local)


def lead_kernel(keep_ref, info_ref, x_ref, parent_ref, o_ref):
    first = (info_ref[1] == 1).astype(jnp.float32)
    for row in range(ROWS):
        keep = keep_ref[row].astype(jnp.float32)
        for group in range(GROUPS):
            front, col = group // COLS, group % COLS
            tile = slice(group * 8, group * 8 + 8)
            o_ref[front, row, col, 0:8] = x_ref[row * BLK + group * 8 : row * BLK + group * 8 + 8, :] * keep
            for j in range(2):
                place = 2 * row + j
                p, q = place // WB, place % WB
                here = keep_ref[0] * (info_ref[0] == place).astype(jnp.int32)
                part = x_ref[tile, :] * here.astype(jnp.float32)
                extra = parent_ref[p * BLK + group * 8 : p * BLK + group * 8 + 8, q * BLK : (q + 1) * BLK]
                o_ref[front, row, col, 8 + 8 * j : 16 + 8 * j] = part + extra * first


def make_lead(keep, info, local, parent):
    return pl.pallas_call(
        lead_kernel,
        name="lead",
        grid_spec=pltpu.PrefetchScalarGridSpec(
            num_scalar_prefetch=2,
            grid=(1,),
            in_specs=[
                pl.BlockSpec((ROWS * BLK, BLK), lambda i, *_: (0, 0)),
                pl.BlockSpec((W, W), lambda i, *_: (0, 0)),
            ],
            out_specs=pl.BlockSpec((FRONTS, ROWS, COLS, 24, BLK), lambda i, *_: (0, 0, 0, 0, 0)),
        ),
        out_shape=jax.ShapeDtypeStruct((FRONTS, ROWS, COLS, 24, BLK), jnp.float32),
    )(keep, info, local, parent)


def slice_kernel(inv_row_ref, inv_lead_ref, recv_ref, parent_ref, o_ref):
    for a in range(PR):
        for q in range(WB):
            total = parent_ref[a, :, q * BLK : (q + 1) * BLK]
            for front in range(FRONTS):
                r = inv_row_ref[front, a]
                c = inv_lead_ref[front, q]
                ok = jnp.logical_and(r >= 0, c >= 0).astype(jnp.float32)
                source = front * 32 + jnp.maximum(r, 0) * COLS + jnp.maximum(c, 0)
                total = total + recv_ref[source, 0:8] * ok
            o_ref[a, :, q * BLK : (q + 1) * BLK] = total


def assemble_slices(inv_row, inv_lead, recv, parent):
    smem = pl.BlockSpec(memory_space=pltpu.SMEM)
    vmem = pl.BlockSpec(memory_space=pltpu.VMEM)
    return pl.pallas_call(
        slice_kernel,
        name="slices",
        in_specs=[smem, smem, vmem, vmem],
        out_specs=vmem,
        out_shape=jax.ShapeDtypeStruct((PR, 8, W), jnp.float32),
    )(inv_row, inv_lead, recv, parent)


KB = 4


def factor_diagonal(get, put):
    groups = BLK // 8
    a = [get(g) for g in range(groups)]
    lanes = lax.broadcasted_iota(jnp.int32, (8, BLK), 1)
    subs = lax.broadcasted_iota(jnp.int32, (8, BLK), 0)
    e = [jnp.where(lanes == subs + 8 * g, 1.0, 0.0).astype(jnp.float32) for g in range(groups)]
    full = (8, BLK)
    for j0 in range(0, BLK, KB):
        g0, i0 = j0 // 8, j0 % 8
        head = [jnp.broadcast_to(a[g0][:, j0 + k : j0 + k + 1], full) for k in range(KB)]
        small = [[None] * KB for _ in range(KB)]
        for i in range(KB):
            for k in range(i + 1):
                small[i][k] = jnp.broadcast_to(head[k][i0 + i : i0 + i + 1, :], full)
        inv = [None] * KB
        low = [[None] * KB for _ in range(KB)]
        for k in range(KB):
            root = lax.rsqrt(small[k][k])
            inv[k] = root * (1.5 - 0.5 * small[k][k] * root * root)
            for i in range(k + 1, KB):
                low[i][k] = small[i][k] * inv[k]
            for i in range(k + 1, KB):
                for m in range(k + 1, i + 1):
                    small[i][m] = small[i][m] - low[i][k] * low[m][k]
        u, w = [], []
        for k in range(KB):
            r = jnp.broadcast_to(a[g0][i0 + k : i0 + k + 1, :], full)
            s = jnp.broadcast_to(e[g0][i0 + k : i0 + k + 1, :], full)
            for m in range(k):
                r = r - low[k][m] * u[m]
                s = s - low[k][m] * w[m]
            u.append(r * inv[k])
            w.append(s * inv[k])
        for g in range(g0, groups):
            if g == g0 and i0 + KB == 8:
                pass
            else:
                mult = []
                for k in range(KB):
                    c = head[k] if g == g0 else jnp.broadcast_to(a[g][:, j0 + k : j0 + k + 1], full)
                    for m in range(k):
                        c = c - mult[m] * low[k][m]
                    mult.append(c * inv[k])
                if g == g0:
                    mult = [jnp.where(subs >= i0 + KB, c, 0.0) for c in mult]
                for k in range(KB):
                    a[g] = a[g] - mult[k] * u[k]
                    e[g] = e[g] - mult[k] * w[k]
            if g == g0:
                for k in range(KB):
                    e[g] = jnp.where(subs == i0 + k, w[k], e[g])
        if i0 + KB == 8:
            put(g0, e[g0])


def factor_kernel(x_ref, high_ref, low_ref, m_ref, d_ref):
    for source in range(FRONTS * ROWS * COLS):
        row = source // COLS % ROWS
        group = source // 32 * COLS + source % COLS
        for j in range(2):
            p, q = (2 * row + j) // WB, (2 * row + j) % WB
            m_ref[p * BLK + group * 8 : p * BLK + group * 8 + 8, q * BLK : (q + 1) * BLK] = x_ref[
                source, 8 * j : 8 * j + 8
            ]
    lanes = lax.broadcasted_iota(jnp.int32, (BLK, BLK), 1)
    subs = lax.broadcasted_iota(jnp.int32, (BLK, BLK), 0)
    eye = jnp.where(lanes == subs, 1.0, 0.0).astype(jnp.float32)
    m_ref[:, W:] = jnp.zeros((W, W), jnp.float32)
    for block in range(W // BLK):
        m_ref[block * BLK : (block + 1) * BLK, W + block * BLK : W + (block + 1) * BLK] = eye

    def step(block, carry):
        base = pl.multiple_of(block * BLK, BLK)

        def get(g):
            return m_ref[pl.ds(pl.multiple_of(base + g * 8, 8), 8), pl.ds(base, BLK)]

        def put(g, value):
            d_ref[g * 8 : (g + 1) * 8, :] = value

        factor_diagonal(get, put)
        rows = jnp.dot(
            d_ref[...], m_ref[pl.ds(base, BLK), :], precision=HIGHEST, preferred_element_type=jnp.float32
        )
        m_ref[pl.ds(base, BLK), :] = rows

        @pl.when(block < W // BLK - 1)
        def _():
            column = lax.broadcasted_iota(jnp.int32, (BLK, W), 1)
            later = jnp.where(column >= base + BLK, rows[:, :W], 0.0)
            m_ref[...] = m_ref[...] - lax.dot_general(
                later, rows, (((0,), (0,)), ((), ())), precision=HIGHEST, preferred_element_type=jnp.float32
            )

        return carry

    lax.fori_loop(0, W // BLK, step, 0)
    inverse = m_ref[:, W:]
    high = inverse.astype(jnp.bfloat16)
    high_ref[...] = high
    low_ref[...] = (inverse - high.astype(jnp.float32)).astype(jnp.bfloat16)


def factor_inverse(tiles):
    vmem = pl.BlockSpec(memory_space=pltpu.VMEM)
    half = jax.ShapeDtypeStruct((W, W), jnp.bfloat16)
    return pl.pallas_call(
        factor_kernel,
        name="factor",
        in_specs=[vmem],
        out_specs=[vmem, vmem],
        out_shape=[half, half],
        scratch_shapes=[pltpu.VMEM((W, 2 * W), jnp.float32), pltpu.VMEM((BLK, BLK), jnp.float32)],
        compiler_params=pltpu.CompilerParams(vmem_limit_bytes=40 << 20),
    )(tiles)


def split(x):
    high = x.astype(jnp.bfloat16)
    return high, (x - high.astype(jnp.float32)).astype(jnp.bfloat16)


def three_products(x, high, low):
    def product(a, b):
        return lax.dot_general(a, b, (((1,), (1,)), ((), ())), preferred_element_type=jnp.float32)

    x_high, x_low = split(x)
    return (product(x_high, low) + product(x_low, high)) + product(x_high, high)


def panel_kernel(place_ref, rows_ref, *refs):
    cols = refs[:4]
    inverse_high, inverse_low, panel_ref, high_ref, low_ref, block_ref = refs[4:]
    step = pl.program_id(0)

    def times_inverse(x):
        return three_products(x, inverse_high[...], inverse_low[...])

    @pl.when(step < PR)
    def _():
        panel_ref[...] = times_inverse(rows_ref[:, 0].reshape(BLK, W))

    @pl.when(step >= PR)
    def _():
        for other in range(4):
            for slot in range(2):
                source = place_ref[0] ^ (slot * 4 + other)
                start = pl.multiple_of(source * 16, 16)
                block_ref[pl.ds(start, 16), :] = cols[other][slot, 0]
        value = times_inverse(block_ref[...])
        high_ref[...], low_ref[...] = split(value)


def make_panels(place, rows_raw, cols_raw, inverses):
    def in_rows(i):
        return jnp.minimum(i, PR - 1)

    def in_cols(i):
        return jnp.maximum(i - PR, 0)

    half = jax.ShapeDtypeStruct((PC * BLK, W), jnp.bfloat16)
    return pl.pallas_call(
        panel_kernel,
        name="panels",
        grid_spec=pltpu.PrefetchScalarGridSpec(
            num_scalar_prefetch=1,
            grid=(PR + PC,),
            in_specs=[pl.BlockSpec((GROUPS, 1, 8, W), lambda i, p: (0, in_rows(i), 0, 0))]
            + [pl.BlockSpec((2, 1, 16, W), lambda i, p: (0, in_cols(i), 0, 0))] * 4
            + [pl.BlockSpec((W, W), lambda i, p: (0, 0))] * 2,
            out_specs=[
                pl.BlockSpec((BLK, W), lambda i, p: (in_rows(i), 0)),
                pl.BlockSpec((BLK, W), lambda i, p: (in_cols(i), 0)),
                pl.BlockSpec((BLK, W), lambda i, p: (in_cols(i), 0)),
            ],
            scratch_shapes=[pltpu.VMEM((BLK, W), jnp.float32)],
        ),
        out_shape=[jax.ShapeDtypeStruct((PR * BLK, W), jnp.float32), half, half],
        compiler_params=pltpu.CompilerParams(vmem_limit_bytes=32 << 20),
    )(place, rows_raw, *cols_raw, *inverses)


def final_kernel(inv_row_ref, inv_col_ref, lead_ref, *refs):
    recvs = refs[:FRONTS]
    parent_ref, panel_ref, high_ref, low_ref, o_ref = refs[FRONTS:]
    a = pl.program_id(0)
    o_ref[...] = parent_ref[...] - three_products(panel_ref[...], high_ref[...], low_ref[...])
    for b in range(PC):
        span = slice(b * BLK, (b + 1) * BLK)
        total = o_ref[:, span]
        for front in range(FRONTS):
            r = inv_row_ref[front, a]
            c = inv_col_ref[front, b]
            ok = jnp.logical_and(r >= 0, c >= 0).astype(jnp.float32)
            total = total + recvs[front][jnp.maximum(c, 0)] * ok
        o_ref[:, span] = total
    leading_row = jnp.logical_and(lead_ref[0] == 1, a < WB)

    @pl.when(leading_row)
    def _():
        o_ref[...] = jnp.zeros_like(o_ref)

    @pl.when(lead_ref[1] == 1)
    def _():
        o_ref[:, :W] = jnp.zeros((BLK, W), jnp.float32)


def finish(inv_row, inv_col, lead, recv, parent, panel, high, low):
    def recv_map(front):
        return lambda a, ir, ic, ld: (front * ROWS + jnp.maximum(ir[front, a], 0), 0, 0)

    whole = pl.BlockSpec((PC * BLK, W), lambda a, *_: (0, 0))
    return pl.pallas_call(
        final_kernel,
        name="finish",
        grid_spec=pltpu.PrefetchScalarGridSpec(
            num_scalar_prefetch=3,
            grid=(PR,),
            in_specs=[
                pl.BlockSpec((COLS, BLK, BLK), recv_map(front)) for front in range(FRONTS)
            ]
            + [
                pl.BlockSpec((BLK, PC * BLK), lambda a, *_: (a, 0)),
                pl.BlockSpec((BLK, W), lambda a, *_: (a, 0)),
                whole,
                whole,
            ],
            out_specs=pl.BlockSpec((BLK, PC * BLK), lambda a, *_: (a, 0)),
        ),
        out_shape=jax.ShapeDtypeStruct((PR * BLK, PC * BLK), jnp.float32),
        compiler_params=pltpu.CompilerParams(vmem_limit_bytes=40 << 20),
    )(inv_row, inv_col, lead, recv, recv, recv, recv, parent, panel, high, low)


def inverse_places(places, length):
    count = places.shape[1]
    hits = places[:, :, None] == jnp.arange(length, dtype=jnp.int32)
    order = jnp.arange(1, count + 1, dtype=jnp.int32)[None, :, None]
    return jnp.sum(jnp.where(hits, order, 0), axis=1) - 1


def scatter_from_first(x, axis, parts):
    index = lax.axis_index(axis)
    total = jnp.where(index == 0, parts(x, 0), 0.0)
    for k in range(1, lax.axis_size(axis)):
        total = total + lax.ppermute(parts(x, k), axis, [(0, k)])
    return total


def flipped(x, axis, bits):
    size = lax.axis_size(axis)
    return lax.ppermute(x, axis, [(i, i ^ bits) for i in range(size)])


def swap_pairs(flip):
    pairs = []
    for front in range(FRONTS):
        for row in range(ROWS):
            for col in range(COLS):
                group = front * COLS + col
                half = group % 2 if flip == 0 else 1 - group % 2
                to_row, to_group = group // 2, 2 * row + half
                target = (to_group // COLS) * 32 + to_row * COLS + to_group % COLS
                pairs.append((front * 32 + row * COLS + col, target))
    return pairs


def body(parent_entries, child_update, child_map, child_mask):
    row = lax.axis_index("row")
    front = lax.axis_index("front")
    col = lax.axis_index("col")
    group = front * COLS + col
    local = child_update[0]
    window = lax.dynamic_slice(child_mask[0], (row * ROWS, col * GROUPS), (ROWS, GROUPS))

    lead_map = child_map.reshape(FRONTS, COLS, GROUPS)[:, :, 0]
    mine = lax.dynamic_index_in_dim(lead_map, front, 0, keepdims=False)
    p = lax.dynamic_index_in_dim(mine, row // 2, 0, keepdims=False)
    q = lax.dynamic_index_in_dim(mine, col, 0, keepdims=False)
    inside = (row % 2 == 0) & (p < WB) & (q < WB)
    corner_place = jnp.where(inside, p * WB + q, -1)
    holder = (row == 0) & (group == 0)
    info = jnp.stack([corner_place, holder.astype(jnp.int32)]).astype(jnp.int32)
    lead = make_lead(window[:, 0], info, local, parent_entries).reshape(128, 24, BLK)
    lead_recv = lax.all_to_all(lead, ALL, 0, 0, tiled=True)
    tiles = jnp.sum(lead_recv[:, 8:], axis=0)
    tiles = jnp.broadcast_to(tiles[None], (128, 16, BLK))
    tiles = lax.all_to_all(tiles, ALL, 0, 0, tiled=True)
    inverses = factor_inverse(tiles)

    first = parent_entries[:, :W].reshape(PR, FRONTS, COLS, 8, W)
    first = scatter_from_first(first, "col", lambda x, k: x[:, :, k])
    first = scatter_from_first(first, "front", lambda x, k: x[:, k])

    column = group // 2 + 8 * (group % 2)
    by_row = lax.dynamic_index_in_dim(child_map.reshape(FRONTS, ROWS, 8), row, 2, keepdims=False)
    by_col = lax.dynamic_index_in_dim(
        child_map.reshape(FRONTS, COLS, GROUPS), column, 2, keepdims=False
    )
    inv_row = inverse_places(by_row - row * PR, PR)
    inv_col = inverse_places(by_col - group * PC, PC)
    inv_lead = inverse_places(lead_map, WB)

    slices = assemble_slices(inv_row, inv_lead, lead_recv, first)

    place = jnp.stack([row, group]).astype(jnp.int32)

    rows_raw = lax.all_gather(slices.reshape(PR * 8, W), GRP, axis=0, tiled=True)
    rows_raw = rows_raw.reshape(GROUPS, PR, 8, W)

    even = group % 2 == 0
    one = lax.ppermute(jnp.where(even, slices[:PC], slices[PC:]), ALL, swap_pairs(0))
    two = lax.ppermute(jnp.where(even, slices[PC:], slices[:PC]), ALL, swap_pairs(1))
    mine = jnp.stack([jnp.where(even, one, two), jnp.where(even, two, one)], axis=1)
    mine = mine.reshape(PC, 16, W)
    mine = jnp.stack([mine, flipped(mine, "row", 4)])
    cols_raw = [mine] + [flipped(mine, "row", bits) for bits in range(1, 4)]

    packed = pack(window, local).reshape(128, BLK, BLK)
    packed, cols_raw = lax.optimization_barrier((packed, cols_raw))
    recv = lax.all_to_all(packed, ALL, 0, 0, tiled=True)

    panel, high, low = make_panels(place, rows_raw, cols_raw, inverses)
    lead_flags = jnp.stack([row == 0, group == 0]).astype(jnp.int32)
    schur = finish(inv_row, inv_col, lead_flags, recv, parent_entries, panel, high, low)
    return schur, panel


def solution(mesh):
    placed = (P("row", ("front", "col")), P("front", "row", "col"), P(), P("front", None, None))
    return jax.shard_map(
        body,
        mesh=mesh,
        in_specs=placed,
        out_specs=(P("row", ("front", "col")), P("row", None)),
        check_vma=False,
    )
```

```python
import functools

import jax
import jax.numpy as jnp
from jax import lax
from jax.experimental import pallas as pl
from jax.experimental.pallas import tpu as pltpu
from jax.sharding import PartitionSpec as P

W = 512
BLK = 128
FRONTS = 4
ROWS = 8
COLS = 4
GROUPS = 16
PR = 12
PC = 6
WB = W // BLK
ALL = ("front", "row", "col")
GRP = ("front", "col")
HIGHEST = lax.Precision.HIGHEST


def group_column(group):
    return group // 2 + 8 * (group % 2)


def pack_kernel(mask_ref, x_ref, o_ref):
    step = pl.program_id(0)
    for front in range(FRONTS):
        for col in range(COLS):
            v = group_column(front * COLS + col)
            keep = mask_ref[step, v].astype(jnp.float32)
            o_ref[front, 0, col] = x_ref[:, v * BLK : (v + 1) * BLK] * keep


def pack(window, local):
    return pl.pallas_call(
        pack_kernel,
        name="pack",
        grid_spec=pltpu.PrefetchScalarGridSpec(
            num_scalar_prefetch=1,
            grid=(ROWS,),
            in_specs=[pl.BlockSpec((BLK, GROUPS * BLK), lambda i, m: (i, 0))],
            out_specs=pl.BlockSpec(
                (FRONTS, 1, COLS, BLK, BLK), lambda i, m: (0, i, 0, 0, 0)
            ),
        ),
        out_shape=jax.ShapeDtypeStruct((FRONTS, ROWS, COLS, BLK, BLK), jnp.float32),
        compiler_params=pltpu.CompilerParams(vmem_limit_bytes=32 << 20),
    )(window, local)


def lead_kernel(keep_ref, info_ref, x_ref, parent_ref, o_ref):
    first = (info_ref[1] == 1).astype(jnp.float32)
    for row in range(ROWS):
        keep = keep_ref[row].astype(jnp.float32)
        for group in range(GROUPS):
            front, col = group // COLS, group % COLS
            tile = slice(group * 8, group * 8 + 8)
            o_ref[front, row, col, 0:8] = x_ref[row * BLK + group * 8 : row * BLK + group * 8 + 8, :] * keep
            for j in range(2):
                place = 2 * row + j
                p, q = place // WB, place % WB
                here = keep_ref[0] * (info_ref[0] == place).astype(jnp.int32)
                part = x_ref[tile, :] * here.astype(jnp.float32)
                extra = parent_ref[p * BLK + group * 8 : p * BLK + group * 8 + 8, q * BLK : (q + 1) * BLK]
                o_ref[front, row, col, 8 + 8 * j : 16 + 8 * j] = part + extra * first


def make_lead(keep, info, local, parent):
    return pl.pallas_call(
        lead_kernel,
        name="lead",
        grid_spec=pltpu.PrefetchScalarGridSpec(
            num_scalar_prefetch=2,
            grid=(1,),
            in_specs=[
                pl.BlockSpec((ROWS * BLK, BLK), lambda i, *_: (0, 0)),
                pl.BlockSpec((W, W), lambda i, *_: (0, 0)),
            ],
            out_specs=pl.BlockSpec((FRONTS, ROWS, COLS, 24, BLK), lambda i, *_: (0, 0, 0, 0, 0)),
        ),
        out_shape=jax.ShapeDtypeStruct((FRONTS, ROWS, COLS, 24, BLK), jnp.float32),
    )(keep, info, local, parent)


def slice_kernel(inv_row_ref, inv_lead_ref, recv_ref, parent_ref, o_ref):
    for a in range(PR):
        for q in range(WB):
            total = parent_ref[a, :, q * BLK : (q + 1) * BLK]
            for front in range(FRONTS):
                r = inv_row_ref[front, a]
                c = inv_lead_ref[front, q]
                ok = jnp.logical_and(r >= 0, c >= 0).astype(jnp.float32)
                source = front * 32 + jnp.maximum(r, 0) * COLS + jnp.maximum(c, 0)
                total = total + recv_ref[source, 0:8] * ok
            o_ref[a, :, q * BLK : (q + 1) * BLK] = total


def assemble_slices(inv_row, inv_lead, recv, parent):
    smem = pl.BlockSpec(memory_space=pltpu.SMEM)
    vmem = pl.BlockSpec(memory_space=pltpu.VMEM)
    return pl.pallas_call(
        slice_kernel,
        name="slices",
        in_specs=[smem, smem, vmem, vmem],
        out_specs=vmem,
        out_shape=jax.ShapeDtypeStruct((PR, 8, W), jnp.float32),
    )(inv_row, inv_lead, recv, parent)


KB = 4


def factor_diagonal(get, put):
    groups = BLK // 8
    a = [get(g) for g in range(groups)]
    lanes = lax.broadcasted_iota(jnp.int32, (8, BLK), 1)
    subs = lax.broadcasted_iota(jnp.int32, (8, BLK), 0)
    e = [jnp.where(lanes == subs + 8 * g, 1.0, 0.0).astype(jnp.float32) for g in range(groups)]
    full = (8, BLK)
    for j0 in range(0, BLK, KB):
        g0, i0 = j0 // 8, j0 % 8
        head = [jnp.broadcast_to(a[g0][:, j0 + k : j0 + k + 1], full) for k in range(KB)]
        small = [[None] * KB for _ in range(KB)]
        for i in range(KB):
            for k in range(i + 1):
                small[i][k] = jnp.broadcast_to(head[k][i0 + i : i0 + i + 1, :], full)
        inv = [None] * KB
        low = [[None] * KB for _ in range(KB)]
        for k in range(KB):
            root = lax.rsqrt(small[k][k])
            inv[k] = root * (1.5 - 0.5 * small[k][k] * root * root)
            for i in range(k + 1, KB):
                low[i][k] = small[i][k] * inv[k]
            for i in range(k + 1, KB):
                for m in range(k + 1, i + 1):
                    small[i][m] = small[i][m] - low[i][k] * low[m][k]
        u, w = [], []
        for k in range(KB):
            r = jnp.broadcast_to(a[g0][i0 + k : i0 + k + 1, :], full)
            s = jnp.broadcast_to(e[g0][i0 + k : i0 + k + 1, :], full)
            for m in range(k):
                r = r - low[k][m] * u[m]
                s = s - low[k][m] * w[m]
            u.append(r * inv[k])
            w.append(s * inv[k])
        for g in range(g0, groups):
            if g == g0 and i0 + KB == 8:
                pass
            else:
                mult = []
                for k in range(KB):
                    c = head[k] if g == g0 else jnp.broadcast_to(a[g][:, j0 + k : j0 + k + 1], full)
                    for m in range(k):
                        c = c - mult[m] * low[k][m]
                    mult.append(c * inv[k])
                if g == g0:
                    mult = [jnp.where(subs >= i0 + KB, c, 0.0) for c in mult]
                for k in range(KB):
                    a[g] = a[g] - mult[k] * u[k]
                    e[g] = e[g] - mult[k] * w[k]
            if g == g0:
                for k in range(KB):
                    e[g] = jnp.where(subs == i0 + k, w[k], e[g])
        if i0 + KB == 8:
            put(g0, e[g0])


def factor_kernel(x_ref, high_ref, low_ref, m_ref, d_ref):
    for source in range(FRONTS * ROWS * COLS):
        row = source // COLS % ROWS
        group = source // 32 * COLS + source % COLS
        for j in range(2):
            p, q = (2 * row + j) // WB, (2 * row + j) % WB
            m_ref[p * BLK + group * 8 : p * BLK + group * 8 + 8, q * BLK : (q + 1) * BLK] = x_ref[
                source, 8 * j : 8 * j + 8
            ]
    lanes = lax.broadcasted_iota(jnp.int32, (BLK, BLK), 1)
    subs = lax.broadcasted_iota(jnp.int32, (BLK, BLK), 0)
    eye = jnp.where(lanes == subs, 1.0, 0.0).astype(jnp.float32)
    m_ref[:, W:] = jnp.zeros((W, W), jnp.float32)
    for block in range(W // BLK):
        m_ref[block * BLK : (block + 1) * BLK, W + block * BLK : W + (block + 1) * BLK] = eye

    def step(block, carry):
        base = pl.multiple_of(block * BLK, BLK)

        def get(g):
            return m_ref[pl.ds(pl.multiple_of(base + g * 8, 8), 8), pl.ds(base, BLK)]

        def put(g, value):
            d_ref[g * 8 : (g + 1) * 8, :] = value

        factor_diagonal(get, put)
        rows = jnp.dot(
            d_ref[...], m_ref[pl.ds(base, BLK), :], precision=HIGHEST, preferred_element_type=jnp.float32
        )
        m_ref[pl.ds(base, BLK), :] = rows

        @pl.when(block < W // BLK - 1)
        def _():
            column = lax.broadcasted_iota(jnp.int32, (BLK, W), 1)
            later = jnp.where(column >= base + BLK, rows[:, :W], 0.0)
            m_ref[...] = m_ref[...] - lax.dot_general(
                later, rows, (((0,), (0,)), ((), ())), precision=HIGHEST, preferred_element_type=jnp.float32
            )

        return carry

    lax.fori_loop(0, W // BLK, step, 0)
    inverse = m_ref[:, W:]
    high = inverse.astype(jnp.bfloat16)
    high_ref[...] = high
    low_ref[...] = (inverse - high.astype(jnp.float32)).astype(jnp.bfloat16)


def factor_inverse(tiles):
    vmem = pl.BlockSpec(memory_space=pltpu.VMEM)
    half = jax.ShapeDtypeStruct((W, W), jnp.bfloat16)
    return pl.pallas_call(
        factor_kernel,
        name="factor",
        in_specs=[vmem],
        out_specs=[vmem, vmem],
        out_shape=[half, half],
        scratch_shapes=[pltpu.VMEM((W, 2 * W), jnp.float32), pltpu.VMEM((BLK, BLK), jnp.float32)],
        compiler_params=pltpu.CompilerParams(vmem_limit_bytes=40 << 20),
    )(tiles)


def split(x):
    high = x.astype(jnp.bfloat16)
    return high, (x - high.astype(jnp.float32)).astype(jnp.bfloat16)


def three_products(x, high, low):
    def product(a, b):
        return lax.dot_general(a, b, (((1,), (1,)), ((), ())), preferred_element_type=jnp.float32)

    x_high, x_low = split(x)
    return (product(x_high, low) + product(x_low, high)) + product(x_high, high)


def panel_kernel(place_ref, *refs):
    rows, cols = refs[:8], refs[8:16]
    inverse_high, inverse_low, panel_ref, high_ref, low_ref, block_ref = refs[16:]
    step = pl.program_id(0)

    def times_inverse(x):
        return three_products(x, inverse_high[...], inverse_low[...])

    @pl.when(step < PR)
    def _():
        for core in range(2):
            for col in range(COLS):
                for x in range(2):
                    source = place_ref[1] ^ (x * 8 + core * 4 + col)
                    start = pl.multiple_of(source * 8, 8)
                    block_ref[pl.ds(start, 8), :] = rows[core * COLS + col][x, 0]
        panel_ref[...] = times_inverse(block_ref[...])

    @pl.when(step >= PR)
    def _():
        for other in range(ROWS):
            start = pl.multiple_of((place_ref[0] ^ other) * 16, 16)
            block_ref[pl.ds(start, 16), :] = cols[other][0]
        value = times_inverse(block_ref[...])
        high_ref[...], low_ref[...] = split(value)


def make_panels(place, rows_raw, cols_raw, inverses):
    def in_rows(i):
        return jnp.minimum(i, PR - 1)

    def in_cols(i):
        return jnp.maximum(i - PR, 0)

    half = jax.ShapeDtypeStruct((PC * BLK, W), jnp.bfloat16)
    return pl.pallas_call(
        panel_kernel,
        name="panels",
        grid_spec=pltpu.PrefetchScalarGridSpec(
            num_scalar_prefetch=1,
            grid=(PR + PC,),
            in_specs=[pl.BlockSpec((2, 1, 8, W), lambda i, p: (0, in_rows(i), 0, 0))] * 8
            + [pl.BlockSpec((1, 16, W), lambda i, p: (in_cols(i), 0, 0))] * ROWS
            + [pl.BlockSpec((W, W), lambda i, p: (0, 0))] * 2,
            out_specs=[
                pl.BlockSpec((BLK, W), lambda i, p: (in_rows(i), 0)),
                pl.BlockSpec((BLK, W), lambda i, p: (in_cols(i), 0)),
                pl.BlockSpec((BLK, W), lambda i, p: (in_cols(i), 0)),
            ],
            scratch_shapes=[pltpu.VMEM((BLK, W), jnp.float32)],
        ),
        out_shape=[jax.ShapeDtypeStruct((PR * BLK, W), jnp.float32), half, half],
        compiler_params=pltpu.CompilerParams(vmem_limit_bytes=32 << 20),
    )(place, *rows_raw, *cols_raw, *inverses)


PAIR = 2


def final_kernel(inv_row_ref, inv_col_ref, lead_ref, *refs):
    recvs = refs[: PAIR * FRONTS]
    parent_ref, panel_ref, high_ref, low_ref, o_ref = refs[PAIR * FRONTS :]
    step = pl.program_id(0)
    o_ref[...] = parent_ref[...] - three_products(panel_ref[...], high_ref[...], low_ref[...])
    for half in range(PAIR):
        rows = slice(half * BLK, (half + 1) * BLK)
        for b in range(PC):
            span = slice(b * BLK, (b + 1) * BLK)
            total = o_ref[rows, span]
            for front in range(FRONTS):
                r = inv_row_ref[front, step * PAIR + half]
                c = inv_col_ref[front, b]
                ok = jnp.logical_and(r >= 0, c >= 0).astype(jnp.float32)
                total = total + recvs[half * FRONTS + front][jnp.maximum(c, 0)] * ok
            o_ref[rows, span] = total

    @pl.when(jnp.logical_and(lead_ref[0] == 1, step < WB // PAIR))
    def _():
        o_ref[...] = jnp.zeros_like(o_ref)

    @pl.when(lead_ref[1] == 1)
    def _():
        o_ref[:, :W] = jnp.zeros((PAIR * BLK, W), jnp.float32)


def finish(inv_row, inv_col, lead, recv, parent, panel, high, low):
    def recv_map(half, front):
        return lambda i, ir, ic, ld: (
            front * ROWS + jnp.maximum(ir[front, i * PAIR + half], 0),
            0,
            0,
        )

    whole = pl.BlockSpec((PC * BLK, W), lambda a, *_: (0, 0))
    block = pl.BlockSpec((PAIR * BLK, PC * BLK), lambda a, *_: (a, 0))
    recv_specs = [
        pl.BlockSpec((COLS, BLK, BLK), recv_map(half, front))
        for half in range(PAIR)
        for front in range(FRONTS)
    ]
    return pl.pallas_call(
        final_kernel,
        name="finish",
        grid_spec=pltpu.PrefetchScalarGridSpec(
            num_scalar_prefetch=3,
            grid=(PR // PAIR,),
            in_specs=recv_specs
            + [block, pl.BlockSpec((PAIR * BLK, W), lambda a, *_: (a, 0)), whole, whole],
            out_specs=block,
        ),
        out_shape=jax.ShapeDtypeStruct((PR * BLK, PC * BLK), jnp.float32),
        compiler_params=pltpu.CompilerParams(vmem_limit_bytes=40 << 20),
    )(inv_row, inv_col, lead, *([recv] * len(recv_specs)), parent, panel, high, low)


def inverse_places(places, length):
    count = places.shape[1]
    hits = places[:, :, None] == jnp.arange(length, dtype=jnp.int32)
    order = jnp.arange(1, count + 1, dtype=jnp.int32)[None, :, None]
    return jnp.sum(jnp.where(hits, order, 0), axis=1) - 1


def flipped(x, axis, bits):
    size = lax.axis_size(axis)
    return lax.ppermute(x, axis, [(i, i ^ bits) for i in range(size)])


def swap_pairs(flip):
    pairs = []
    for front in range(FRONTS):
        for row in range(ROWS):
            for col in range(COLS):
                group = front * COLS + col
                half = group % 2 if flip == 0 else 1 - group % 2
                to_row, to_group = group // 2, 2 * row + half
                target = (to_group // COLS) * 32 + to_row * COLS + to_group % COLS
                pairs.append((front * 32 + row * COLS + col, target))
    return pairs


def body(parent_entries, child_update, child_map, child_mask):
    row = lax.axis_index("row")
    front = lax.axis_index("front")
    col = lax.axis_index("col")
    group = front * COLS + col
    local = child_update[0]
    window = lax.dynamic_slice(child_mask[0], (row * ROWS, col * GROUPS), (ROWS, GROUPS))

    lead_map = child_map.reshape(FRONTS, COLS, GROUPS)[:, :, 0]
    mine = lax.dynamic_index_in_dim(lead_map, front, 0, keepdims=False)
    p = lax.dynamic_index_in_dim(mine, row // 2, 0, keepdims=False)
    q = lax.dynamic_index_in_dim(mine, col, 0, keepdims=False)
    inside = (row % 2 == 0) & (p < WB) & (q < WB)
    corner_place = jnp.where(inside, p * WB + q, -1)
    holder = (row == 0) & (group == 0)
    info = jnp.stack([corner_place, holder.astype(jnp.int32)]).astype(jnp.int32)

    first = parent_entries[:, :W].reshape(PR, FRONTS, COLS, 8, W)
    sent = [lax.ppermute(first[:, :, k], "col", [(0, k)]) for k in range(1, COLS)]
    sent[-1], info = lax.optimization_barrier((sent[-1], info))
    first = jnp.where(col == 0, first[:, :, 0], (sent[0] + sent[1]) + sent[2])
    sent = [lax.ppermute(first[:, k], "front", [(0, k)]) for k in range(1, FRONTS)]
    first = jnp.where(front == 0, first[:, 0], (sent[0] + sent[1]) + sent[2])

    lead = make_lead(window[:, 0], info, local, parent_entries).reshape(128, 24, BLK)
    lead_recv = lax.all_to_all(lead, ALL, 0, 0, tiled=True)
    tiles = jnp.sum(lead_recv[:, 8:], axis=0)
    tiles = jnp.broadcast_to(tiles[None], (128, 16, BLK))
    tiles = lax.all_to_all(tiles, ALL, 0, 0, tiled=True)
    inverses = factor_inverse(tiles)

    column = group // 2 + 8 * (group % 2)
    by_row = lax.dynamic_index_in_dim(child_map.reshape(FRONTS, ROWS, 8), row, 2, keepdims=False)
    by_col = lax.dynamic_index_in_dim(
        child_map.reshape(FRONTS, COLS, GROUPS), column, 2, keepdims=False
    )
    inv_row = inverse_places(by_row - row * PR, PR)
    inv_col = inverse_places(by_col - group * PC, PC)
    inv_lead = inverse_places(lead_map, WB)

    slices = assemble_slices(inv_row, inv_lead, lead_recv, first)

    place = jnp.stack([row, group]).astype(jnp.int32)

    pair = jnp.stack([slices, flipped(slices, "front", 2)])
    pair = [pair] + [flipped(pair, "col", bits) for bits in range(1, COLS)]
    rows_raw = pair + [flipped(x, "front", 1) for x in pair]

    even = group % 2 == 0
    one = lax.ppermute(jnp.where(even, slices[:PC], slices[PC:]), ALL, swap_pairs(0))
    two = lax.ppermute(jnp.where(even, slices[PC:], slices[:PC]), ALL, swap_pairs(1))
    mine = jnp.stack([jnp.where(even, one, two), jnp.where(even, two, one)], axis=1)
    mine = mine.reshape(PC, 16, W)
    cols_raw = [mine] + [flipped(mine, "row", bits) for bits in range(1, ROWS)]

    packed = pack(window, local).reshape(128, BLK, BLK)
    packed, cols_raw, rows_raw = lax.optimization_barrier((packed, cols_raw, rows_raw))
    recv = lax.all_to_all(packed, ALL, 0, 0, tiled=True)

    panel, high, low = make_panels(place, rows_raw, cols_raw, inverses)
    lead_flags = jnp.stack([row == 0, group == 0]).astype(jnp.int32)
    schur = finish(inv_row, inv_col, lead_flags, recv, parent_entries, panel, high, low)
    return schur, panel


def solution(mesh):
    placed = (P("row", ("front", "col")), P("front", "row", "col"), P(), P("front", None, None))
    return jax.shard_map(
        body,
        mesh=mesh,
        in_specs=placed,
        out_specs=(P("row", ("front", "col")), P("row", None)),
        check_vma=False,
    )
```

```python
import functools

import jax
import jax.numpy as jnp
from jax import lax
from jax.experimental import pallas as pl
from jax.experimental.pallas import tpu as pltpu
from jax.sharding import PartitionSpec as P

W = 512
BLK = 128
FRONTS = 4
ROWS = 8
COLS = 4
GROUPS = 16
PR = 12
PC = 6
WB = W // BLK
ALL = ("front", "row", "col")
GRP = ("front", "col")
HIGHEST = lax.Precision.HIGHEST


def group_column(group):
    return group // 2 + 8 * (group % 2)


def pack_kernel(mask_ref, x_ref, o_ref):
    step = pl.program_id(0)
    for front in range(FRONTS):
        for col in range(COLS):
            v = group_column(front * COLS + col)
            keep = mask_ref[step, v].astype(jnp.float32)
            o_ref[front, 0, col] = x_ref[:, v * BLK : (v + 1) * BLK] * keep


def pack(window, local):
    return pl.pallas_call(
        pack_kernel,
        name="pack",
        grid_spec=pltpu.PrefetchScalarGridSpec(
            num_scalar_prefetch=1,
            grid=(ROWS,),
            in_specs=[pl.BlockSpec((BLK, GROUPS * BLK), lambda i, m: (i, 0))],
            out_specs=pl.BlockSpec(
                (FRONTS, 1, COLS, BLK, BLK), lambda i, m: (0, i, 0, 0, 0)
            ),
        ),
        out_shape=jax.ShapeDtypeStruct((FRONTS, ROWS, COLS, BLK, BLK), jnp.float32),
        compiler_params=pltpu.CompilerParams(vmem_limit_bytes=32 << 20),
    )(window, local)


def lead_kernel(keep_ref, info_ref, x_ref, parent_ref, o_ref):
    first = (info_ref[1] == 1).astype(jnp.float32)
    for row in range(ROWS):
        keep = keep_ref[row].astype(jnp.float32)
        for group in range(GROUPS):
            front, col = group // COLS, group % COLS
            tile = slice(group * 8, group * 8 + 8)
            o_ref[front, row, col, 0:8] = x_ref[row * BLK + group * 8 : row * BLK + group * 8 + 8, :] * keep
            for j in range(2):
                place = 2 * row + j
                p, q = place // WB, place % WB
                here = keep_ref[0] * (info_ref[0] == place).astype(jnp.int32)
                part = x_ref[tile, :] * here.astype(jnp.float32)
                extra = parent_ref[p * BLK + group * 8 : p * BLK + group * 8 + 8, q * BLK : (q + 1) * BLK]
                o_ref[front, row, col, 8 + 8 * j : 16 + 8 * j] = part + extra * first


def make_lead(keep, info, local, parent):
    return pl.pallas_call(
        lead_kernel,
        name="lead",
        grid_spec=pltpu.PrefetchScalarGridSpec(
            num_scalar_prefetch=2,
            grid=(1,),
            in_specs=[
                pl.BlockSpec((ROWS * BLK, BLK), lambda i, *_: (0, 0)),
                pl.BlockSpec((W, W), lambda i, *_: (0, 0)),
            ],
            out_specs=pl.BlockSpec((FRONTS, ROWS, COLS, 24, BLK), lambda i, *_: (0, 0, 0, 0, 0)),
        ),
        out_shape=jax.ShapeDtypeStruct((FRONTS, ROWS, COLS, 24, BLK), jnp.float32),
    )(keep, info, local, parent)


def slice_kernel(inv_row_ref, inv_lead_ref, recv_ref, parent_ref, o_ref):
    for a in range(PR):
        for q in range(WB):
            total = parent_ref[a, :, q * BLK : (q + 1) * BLK]
            for front in range(FRONTS):
                r = inv_row_ref[front, a]
                c = inv_lead_ref[front, q]
                ok = jnp.logical_and(r >= 0, c >= 0).astype(jnp.float32)
                source = front * 32 + jnp.maximum(r, 0) * COLS + jnp.maximum(c, 0)
                total = total + recv_ref[source, 0:8] * ok
            o_ref[a, :, q * BLK : (q + 1) * BLK] = total


def assemble_slices(inv_row, inv_lead, recv, parent):
    smem = pl.BlockSpec(memory_space=pltpu.SMEM)
    vmem = pl.BlockSpec(memory_space=pltpu.VMEM)
    return pl.pallas_call(
        slice_kernel,
        name="slices",
        in_specs=[smem, smem, vmem, vmem],
        out_specs=vmem,
        out_shape=jax.ShapeDtypeStruct((PR, 8, W), jnp.float32),
    )(inv_row, inv_lead, recv, parent)


KB = 4


def factor_diagonal(get, put):
    groups = BLK // 8
    a = [get(g) for g in range(groups)]
    lanes = lax.broadcasted_iota(jnp.int32, (8, BLK), 1)
    subs = lax.broadcasted_iota(jnp.int32, (8, BLK), 0)
    e = [jnp.where(lanes == subs + 8 * g, 1.0, 0.0).astype(jnp.float32) for g in range(groups)]
    full = (8, BLK)
    for j0 in range(0, BLK, KB):
        g0, i0 = j0 // 8, j0 % 8
        head = [jnp.broadcast_to(a[g0][:, j0 + k : j0 + k + 1], full) for k in range(KB)]
        small = [[None] * KB for _ in range(KB)]
        for i in range(KB):
            for k in range(i + 1):
                small[i][k] = jnp.broadcast_to(head[k][i0 + i : i0 + i + 1, :], full)
        inv = [None] * KB
        low = [[None] * KB for _ in range(KB)]
        for k in range(KB):
            root = lax.rsqrt(small[k][k])
            inv[k] = root * (1.5 - 0.5 * small[k][k] * root * root)
            for i in range(k + 1, KB):
                low[i][k] = small[i][k] * inv[k]
            for i in range(k + 1, KB):
                for m in range(k + 1, i + 1):
                    small[i][m] = small[i][m] - low[i][k] * low[m][k]
        u, w = [], []
        for k in range(KB):
            r = jnp.broadcast_to(a[g0][i0 + k : i0 + k + 1, :], full)
            s = jnp.broadcast_to(e[g0][i0 + k : i0 + k + 1, :], full)
            for m in range(k):
                r = r - low[k][m] * u[m]
                s = s - low[k][m] * w[m]
            u.append(r * inv[k])
            w.append(s * inv[k])
        for g in range(g0, groups):
            if g == g0 and i0 + KB == 8:
                pass
            else:
                mult = []
                for k in range(KB):
                    c = head[k] if g == g0 else jnp.broadcast_to(a[g][:, j0 + k : j0 + k + 1], full)
                    for m in range(k):
                        c = c - mult[m] * low[k][m]
                    mult.append(c * inv[k])
                if g == g0:
                    mult = [jnp.where(subs >= i0 + KB, c, 0.0) for c in mult]
                for k in range(KB):
                    a[g] = a[g] - mult[k] * u[k]
                    e[g] = e[g] - mult[k] * w[k]
            if g == g0:
                for k in range(KB):
                    e[g] = jnp.where(subs == i0 + k, w[k], e[g])
        if i0 + KB == 8:
            put(g0, e[g0])


def factor_kernel(x_ref, high_ref, low_ref, m_ref, d_ref):
    for source in range(FRONTS * ROWS * COLS):
        row = source // COLS % ROWS
        group = source // 32 * COLS + source % COLS
        for j in range(2):
            p, q = (2 * row + j) // WB, (2 * row + j) % WB
            m_ref[p * BLK + group * 8 : p * BLK + group * 8 + 8, q * BLK : (q + 1) * BLK] = x_ref[
                source, 8 * j : 8 * j + 8
            ]
    lanes = lax.broadcasted_iota(jnp.int32, (BLK, BLK), 1)
    subs = lax.broadcasted_iota(jnp.int32, (BLK, BLK), 0)
    eye = jnp.where(lanes == subs, 1.0, 0.0).astype(jnp.float32)
    m_ref[:, W:] = jnp.zeros((W, W), jnp.float32)
    for block in range(W // BLK):
        m_ref[block * BLK : (block + 1) * BLK, W + block * BLK : W + (block + 1) * BLK] = eye

    def step(block, carry):
        base = pl.multiple_of(block * BLK, BLK)

        def get(g):
            return m_ref[pl.ds(pl.multiple_of(base + g * 8, 8), 8), pl.ds(base, BLK)]

        def put(g, value):
            d_ref[g * 8 : (g + 1) * 8, :] = value

        factor_diagonal(get, put)
        rows = jnp.dot(
            d_ref[...], m_ref[pl.ds(base, BLK), :], precision=HIGHEST, preferred_element_type=jnp.float32
        )
        m_ref[pl.ds(base, BLK), :] = rows

        @pl.when(block < W // BLK - 1)
        def _():
            column = lax.broadcasted_iota(jnp.int32, (BLK, W), 1)
            later = jnp.where(column >= base + BLK, rows[:, :W], 0.0)
            m_ref[...] = m_ref[...] - lax.dot_general(
                later, rows, (((0,), (0,)), ((), ())), precision=HIGHEST, preferred_element_type=jnp.float32
            )

        return carry

    lax.fori_loop(0, W // BLK, step, 0)
    inverse = m_ref[:, W:]
    high = inverse.astype(jnp.bfloat16)
    high_ref[...] = high
    low_ref[...] = (inverse - high.astype(jnp.float32)).astype(jnp.bfloat16)


def factor_inverse(tiles):
    vmem = pl.BlockSpec(memory_space=pltpu.VMEM)
    half = jax.ShapeDtypeStruct((W, W), jnp.bfloat16)
    return pl.pallas_call(
        factor_kernel,
        name="factor",
        in_specs=[vmem],
        out_specs=[vmem, vmem],
        out_shape=[half, half],
        scratch_shapes=[pltpu.VMEM((W, 2 * W), jnp.float32), pltpu.VMEM((BLK, BLK), jnp.float32)],
        compiler_params=pltpu.CompilerParams(vmem_limit_bytes=40 << 20),
    )(tiles)


def split(x):
    high = x.astype(jnp.bfloat16)
    return high, (x - high.astype(jnp.float32)).astype(jnp.bfloat16)


def three_products(x, high, low):
    def product(a, b):
        return lax.dot_general(a, b, (((1,), (1,)), ((), ())), preferred_element_type=jnp.float32)

    x_high, x_low = split(x)
    return (product(x_high, low) + product(x_low, high)) + product(x_high, high)


def rows_kernel(rows_ref, high_ref, low_ref, o_ref):
    o_ref[...] = three_products(rows_ref[:, 0].reshape(BLK, W), high_ref[...], low_ref[...])


def make_panel(rows_raw, inverses):
    whole = pl.BlockSpec((W, W), lambda i: (0, 0))
    return pl.pallas_call(
        rows_kernel,
        name="panel",
        grid=(PR,),
        in_specs=[pl.BlockSpec((GROUPS, 1, 8, W), lambda i: (0, i, 0, 0)), whole, whole],
        out_specs=pl.BlockSpec((BLK, W), lambda i: (i, 0)),
        out_shape=jax.ShapeDtypeStruct((PR * BLK, W), jnp.float32),
    )(rows_raw, *inverses)


def cols_kernel(place_ref, *refs):
    pieces = refs[:ROWS]
    inverse_high, inverse_low, high_ref, low_ref, block_ref = refs[ROWS:]
    for other in range(ROWS):
        start = pl.multiple_of((place_ref[0] ^ other) * 16, 16)
        block_ref[pl.ds(start, 16), :] = pieces[other][0]
    high_ref[...], low_ref[...] = split(
        three_products(block_ref[...], inverse_high[...], inverse_low[...])
    )


def make_across(place, pieces, inverses):
    half = jax.ShapeDtypeStruct((PC * BLK, W), jnp.bfloat16)
    whole = pl.BlockSpec((W, W), lambda i, p: (0, 0))
    block = pl.BlockSpec((BLK, W), lambda i, p: (i, 0))
    return pl.pallas_call(
        cols_kernel,
        name="across",
        grid_spec=pltpu.PrefetchScalarGridSpec(
            num_scalar_prefetch=1,
            grid=(PC,),
            in_specs=[pl.BlockSpec((1, 16, W), lambda i, p: (i, 0, 0))] * ROWS + [whole, whole],
            out_specs=[block, block],
            scratch_shapes=[pltpu.VMEM((BLK, W), jnp.float32)],
        ),
        out_shape=[half, half],
    )(place, *pieces, *inverses)


def assemble_kernel(inv_row_ref, inv_col_ref, *refs):
    recvs = refs[:FRONTS]
    parent_ref, o_ref = refs[FRONTS:]
    a = pl.program_id(0)
    for b in range(PC):
        span = slice(b * BLK, (b + 1) * BLK)
        total = parent_ref[:, span]
        for front in range(FRONTS):
            r = inv_row_ref[front, a]
            c = inv_col_ref[front, b]
            ok = jnp.logical_and(r >= 0, c >= 0).astype(jnp.float32)
            total = total + recvs[front][jnp.maximum(c, 0)] * ok
        o_ref[:, span] = total


def assemble(inv_row, inv_col, recv, parent):
    def recv_map(front):
        return lambda a, ir, ic: (front * ROWS + jnp.maximum(ir[front, a], 0), 0, 0)

    block = pl.BlockSpec((BLK, PC * BLK), lambda a, *_: (a, 0))
    return pl.pallas_call(
        assemble_kernel,
        name="assemble",
        grid_spec=pltpu.PrefetchScalarGridSpec(
            num_scalar_prefetch=2,
            grid=(PR,),
            in_specs=[
                pl.BlockSpec((COLS, BLK, BLK), recv_map(front)) for front in range(FRONTS)
            ]
            + [block],
            out_specs=block,
        ),
        out_shape=jax.ShapeDtypeStruct((PR * BLK, PC * BLK), jnp.float32),
        compiler_params=pltpu.CompilerParams(vmem_limit_bytes=32 << 20),
    )(inv_row, inv_col, recv, recv, recv, recv, parent)


def subtract_kernel(place_ref, whole_ref, panel_ref, high_ref, low_ref, o_ref):
    step = pl.program_id(0)
    blocks = o_ref.shape[0] // BLK
    o_ref[...] = whole_ref[...] - three_products(panel_ref[...], high_ref[...], low_ref[...])

    @pl.when(jnp.logical_and(place_ref[0] == 0, step < WB // blocks))
    def _():
        o_ref[...] = jnp.zeros_like(o_ref)

    @pl.when(place_ref[1] == 0)
    def _():
        o_ref[:, :W] = jnp.zeros((o_ref.shape[0], W), jnp.float32)


def subtract(place, whole, panel, high, low):
    tall = 2 * BLK
    block = pl.BlockSpec((tall, PC * BLK), lambda a, p: (a, 0))
    half = pl.BlockSpec((PC * BLK, W), lambda a, p: (0, 0))
    return pl.pallas_call(
        subtract_kernel,
        name="subtract",
        grid_spec=pltpu.PrefetchScalarGridSpec(
            num_scalar_prefetch=1,
            grid=(PR * BLK // tall,),
            in_specs=[block, pl.BlockSpec((tall, W), lambda a, p: (a, 0)), half, half],
            out_specs=block,
        ),
        out_shape=jax.ShapeDtypeStruct((PR * BLK, PC * BLK), jnp.float32),
        input_output_aliases={1: 0},
        compiler_params=pltpu.CompilerParams(vmem_limit_bytes=32 << 20),
    )(place, whole, panel, high, low)


def inverse_places(places, length):
    count = places.shape[1]
    hits = places[:, :, None] == jnp.arange(length, dtype=jnp.int32)
    order = jnp.arange(1, count + 1, dtype=jnp.int32)[None, :, None]
    return jnp.sum(jnp.where(hits, order, 0), axis=1) - 1


def flipped(x, axis, bits):
    size = lax.axis_size(axis)
    return lax.ppermute(x, axis, [(i, i ^ bits) for i in range(size)])


def swap_pairs(flip):
    pairs = []
    for front in range(FRONTS):
        for row in range(ROWS):
            for col in range(COLS):
                group = front * COLS + col
                half = group % 2 if flip == 0 else 1 - group % 2
                to_row, to_group = group // 2, 2 * row + half
                target = (to_group // COLS) * 32 + to_row * COLS + to_group % COLS
                pairs.append((front * 32 + row * COLS + col, target))
    return pairs


def body(parent_entries, child_update, child_map, child_mask):
    row = lax.axis_index("row")
    front = lax.axis_index("front")
    col = lax.axis_index("col")
    group = front * COLS + col
    local = child_update[0]
    window = lax.dynamic_slice(child_mask[0], (row * ROWS, col * GROUPS), (ROWS, GROUPS))

    lead_map = child_map.reshape(FRONTS, COLS, GROUPS)[:, :, 0]
    mine = lax.dynamic_index_in_dim(lead_map, front, 0, keepdims=False)
    p = lax.dynamic_index_in_dim(mine, row // 2, 0, keepdims=False)
    q = lax.dynamic_index_in_dim(mine, col, 0, keepdims=False)
    inside = (row % 2 == 0) & (p < WB) & (q < WB)
    corner_place = jnp.where(inside, p * WB + q, -1)
    holder = (row == 0) & (group == 0)
    info = jnp.stack([corner_place, holder.astype(jnp.int32)]).astype(jnp.int32)
    first = parent_entries[:, :W].reshape(PR, FRONTS, COLS, 8, W)
    sent = [lax.ppermute(first[:, :, k], "col", [(0, k)]) for k in range(1, COLS)]
    sent[-1], info = lax.optimization_barrier((sent[-1], info))
    lead = make_lead(window[:, 0], info, local, parent_entries).reshape(128, 24, BLK)
    lead_recv = lax.all_to_all(lead, ALL, 0, 0, tiled=True)
    first = jnp.where(col == 0, first[:, :, 0], (sent[0] + sent[1]) + sent[2])
    tiles = jnp.sum(lead_recv[:, 8:], axis=0)
    tiles = jnp.broadcast_to(tiles[None], (128, 16, BLK))
    tiles = lax.all_to_all(tiles, ALL, 0, 0, tiled=True)
    sent = [lax.ppermute(first[:, k], "front", [(0, k)]) for k in range(1, FRONTS)]
    first = jnp.where(front == 0, first[:, 0], (sent[0] + sent[1]) + sent[2])

    column = group // 2 + 8 * (group % 2)
    by_row = lax.dynamic_index_in_dim(child_map.reshape(FRONTS, ROWS, 8), row, 2, keepdims=False)
    by_col = lax.dynamic_index_in_dim(
        child_map.reshape(FRONTS, COLS, GROUPS), column, 2, keepdims=False
    )
    inv_row = inverse_places(by_row - row * PR, PR)
    inv_col = inverse_places(by_col - group * PC, PC)
    inv_lead = inverse_places(lead_map, WB)

    slices = assemble_slices(inv_row, inv_lead, lead_recv, first)

    place = jnp.stack([row, group]).astype(jnp.int32)

    even = group % 2 == 0
    one = lax.ppermute(jnp.where(even, slices[:PC], slices[PC:]), ALL, swap_pairs(0))
    two = lax.ppermute(jnp.where(even, slices[PC:], slices[:PC]), ALL, swap_pairs(1))
    mine = jnp.stack([jnp.where(even, one, two), jnp.where(even, two, one)], axis=1)
    mine = mine.reshape(PC, 16, W)

    rows_raw = lax.all_gather(slices.reshape(PR * 8, W), GRP, axis=0, tiled=True)
    rows_raw = rows_raw.reshape(GROUPS, PR, 8, W)

    packed = pack(window, local).reshape(128, BLK, BLK)
    packed, mine, tiles = lax.optimization_barrier((packed, mine, tiles))
    recv = lax.all_to_all(packed, ALL, 0, 0, tiled=True)

    inverses = factor_inverse(tiles)
    mine, *inverses = lax.optimization_barrier((mine, *inverses))
    pieces = [mine] + [flipped(mine, "row", bits) for bits in range(1, ROWS)]
    whole = assemble(inv_row, inv_col, recv, parent_entries)
    *pieces, rows_raw, whole = lax.optimization_barrier((*pieces, rows_raw, whole))
    panel = make_panel(rows_raw, inverses)
    high, low = make_across(place, pieces, inverses)
    schur = subtract(place, whole, panel, high, low)
    return schur, panel


def solution(mesh):
    placed = (P("row", ("front", "col")), P("front", "row", "col"), P(), P("front", None, None))
    return jax.shard_map(
        body,
        mesh=mesh,
        in_specs=placed,
        out_specs=(P("row", ("front", "col")), P("row", None)),
        check_vma=False,
    )
```

```python
import functools

import jax
import jax.numpy as jnp
from jax import lax
from jax.experimental import pallas as pl
from jax.experimental.pallas import tpu as pltpu
from jax.sharding import PartitionSpec as P

W = 512
BLK = 128
HALF = BLK // 2
FRONTS = 4
ROWS = 8
COLS = 4
GROUPS = 16
PR = 12
PC = 6
WB = W // BLK
ALL = ("front", "row", "col")
GRP = ("front", "col")
HIGHEST = lax.Precision.HIGHEST


def group_column(group):
    return group // 2 + 8 * (group % 2)


def pack_kernel(mask_ref, x_ref, upper_ref, lower_ref):
    step = pl.program_id(0)
    for front in range(FRONTS):
        for col in range(COLS):
            v = group_column(front * COLS + col)
            keep = mask_ref[step, v].astype(jnp.float32)
            span = slice(v * BLK, (v + 1) * BLK)
            upper_ref[front, 0, col] = x_ref[:HALF, span] * keep
            lower_ref[front, 0, col] = x_ref[HALF:, span] * keep


def pack(window, local):
    half = jax.ShapeDtypeStruct((FRONTS, ROWS, COLS, HALF, BLK), jnp.float32)
    spec = pl.BlockSpec((FRONTS, 1, COLS, HALF, BLK), lambda i, m: (0, i, 0, 0, 0))
    return pl.pallas_call(
        pack_kernel,
        name="pack",
        grid_spec=pltpu.PrefetchScalarGridSpec(
            num_scalar_prefetch=1,
            grid=(ROWS,),
            in_specs=[pl.BlockSpec((BLK, GROUPS * BLK), lambda i, m: (i, 0))],
            out_specs=[spec, spec],
        ),
        out_shape=[half, half],
        compiler_params=pltpu.CompilerParams(vmem_limit_bytes=32 << 20),
    )(window, local)


def lead_kernel(keep_ref, info_ref, x_ref, parent_ref, o_ref):
    first = (info_ref[1] == 1).astype(jnp.float32)
    for row in range(ROWS):
        keep = keep_ref[row].astype(jnp.float32)
        for group in range(GROUPS):
            front, col = group // COLS, group % COLS
            tile = slice(group * 8, group * 8 + 8)
            o_ref[front, row, col, 0:8] = x_ref[row * BLK + group * 8 : row * BLK + group * 8 + 8, :] * keep
            for j in range(2):
                place = 2 * row + j
                p, q = place // WB, place % WB
                here = keep_ref[0] * (info_ref[0] == place).astype(jnp.int32)
                part = x_ref[tile, :] * here.astype(jnp.float32)
                extra = parent_ref[p * BLK + group * 8 : p * BLK + group * 8 + 8, q * BLK : (q + 1) * BLK]
                o_ref[front, row, col, 8 + 8 * j : 16 + 8 * j] = part + extra * first


def make_lead(keep, info, local, parent):
    return pl.pallas_call(
        lead_kernel,
        name="lead",
        grid_spec=pltpu.PrefetchScalarGridSpec(
            num_scalar_prefetch=2,
            grid=(1,),
            in_specs=[
                pl.BlockSpec((ROWS * BLK, BLK), lambda i, *_: (0, 0)),
                pl.BlockSpec((W, W), lambda i, *_: (0, 0)),
            ],
            out_specs=pl.BlockSpec((FRONTS, ROWS, COLS, 24, BLK), lambda i, *_: (0, 0, 0, 0, 0)),
        ),
        out_shape=jax.ShapeDtypeStruct((FRONTS, ROWS, COLS, 24, BLK), jnp.float32),
    )(keep, info, local, parent)


def slice_kernel(inv_row_ref, inv_lead_ref, recv_ref, parent_ref, o_ref):
    for a in range(PR):
        for q in range(WB):
            total = parent_ref[a, :, q * BLK : (q + 1) * BLK]
            for front in range(FRONTS):
                r = inv_row_ref[front, a]
                c = inv_lead_ref[front, q]
                ok = jnp.logical_and(r >= 0, c >= 0).astype(jnp.float32)
                source = front * 32 + jnp.maximum(r, 0) * COLS + jnp.maximum(c, 0)
                total = total + recv_ref[source, 0:8] * ok
            o_ref[a, :, q * BLK : (q + 1) * BLK] = total


def assemble_slices(inv_row, inv_lead, recv, parent):
    smem = pl.BlockSpec(memory_space=pltpu.SMEM)
    vmem = pl.BlockSpec(memory_space=pltpu.VMEM)
    return pl.pallas_call(
        slice_kernel,
        name="slices",
        in_specs=[smem, smem, vmem, vmem],
        out_specs=vmem,
        out_shape=jax.ShapeDtypeStruct((PR, 8, W), jnp.float32),
    )(inv_row, inv_lead, recv, parent)


KB = 4


def factor_diagonal(get, put):
    groups = BLK // 8
    a = [get(g) for g in range(groups)]
    lanes = lax.broadcasted_iota(jnp.int32, (8, BLK), 1)
    subs = lax.broadcasted_iota(jnp.int32, (8, BLK), 0)
    e = [jnp.where(lanes == subs + 8 * g, 1.0, 0.0).astype(jnp.float32) for g in range(groups)]
    full = (8, BLK)
    for j0 in range(0, BLK, KB):
        g0, i0 = j0 // 8, j0 % 8
        head = [jnp.broadcast_to(a[g0][:, j0 + k : j0 + k + 1], full) for k in range(KB)]
        small = [[None] * KB for _ in range(KB)]
        for i in range(KB):
            for k in range(i + 1):
                small[i][k] = jnp.broadcast_to(head[k][i0 + i : i0 + i + 1, :], full)
        inv = [None] * KB
        low = [[None] * KB for _ in range(KB)]
        for k in range(KB):
            root = lax.rsqrt(small[k][k])
            inv[k] = root * (1.5 - 0.5 * small[k][k] * root * root)
            for i in range(k + 1, KB):
                low[i][k] = small[i][k] * inv[k]
            for i in range(k + 1, KB):
                for m in range(k + 1, i + 1):
                    small[i][m] = small[i][m] - low[i][k] * low[m][k]
        u, w = [], []
        for k in range(KB):
            r = jnp.broadcast_to(a[g0][i0 + k : i0 + k + 1, :], full)
            s = jnp.broadcast_to(e[g0][i0 + k : i0 + k + 1, :], full)
            for m in range(k):
                r = r - low[k][m] * u[m]
                s = s - low[k][m] * w[m]
            u.append(r * inv[k])
            w.append(s * inv[k])
        for g in range(g0, groups):
            if g == g0 and i0 + KB == 8:
                pass
            else:
                mult = []
                for k in range(KB):
                    c = head[k] if g == g0 else jnp.broadcast_to(a[g][:, j0 + k : j0 + k + 1], full)
                    for m in range(k):
                        c = c - mult[m] * low[k][m]
                    mult.append(c * inv[k])
                if g == g0:
                    mult = [jnp.where(subs >= i0 + KB, c, 0.0) for c in mult]
                for k in range(KB):
                    a[g] = a[g] - mult[k] * u[k]
                    e[g] = e[g] - mult[k] * w[k]
            if g == g0:
                for k in range(KB):
                    e[g] = jnp.where(subs == i0 + k, w[k], e[g])
        if i0 + KB == 8:
            put(g0, e[g0])


def factor_kernel(x_ref, high_ref, low_ref, m_ref, d_ref):
    for source in range(FRONTS * ROWS * COLS):
        row = source // COLS % ROWS
        group = source // 32 * COLS + source % COLS
        for j in range(2):
            p, q = (2 * row + j) // WB, (2 * row + j) % WB
            m_ref[p * BLK + group * 8 : p * BLK + group * 8 + 8, q * BLK : (q + 1) * BLK] = x_ref[
                source, 8 * j : 8 * j + 8
            ]
    lanes = lax.broadcasted_iota(jnp.int32, (BLK, BLK), 1)
    subs = lax.broadcasted_iota(jnp.int32, (BLK, BLK), 0)
    eye = jnp.where(lanes == subs, 1.0, 0.0).astype(jnp.float32)
    m_ref[:, W:] = jnp.zeros((W, W), jnp.float32)
    for block in range(W // BLK):
        m_ref[block * BLK : (block + 1) * BLK, W + block * BLK : W + (block + 1) * BLK] = eye

    def step(block, carry):
        base = pl.multiple_of(block * BLK, BLK)

        def get(g):
            return m_ref[pl.ds(pl.multiple_of(base + g * 8, 8), 8), pl.ds(base, BLK)]

        def put(g, value):
            d_ref[g * 8 : (g + 1) * 8, :] = value

        factor_diagonal(get, put)
        rows = jnp.dot(
            d_ref[...], m_ref[pl.ds(base, BLK), :], precision=HIGHEST, preferred_element_type=jnp.float32
        )
        m_ref[pl.ds(base, BLK), :] = rows

        @pl.when(block < W // BLK - 1)
        def _():
            column = lax.broadcasted_iota(jnp.int32, (BLK, W), 1)
            later = jnp.where(column >= base + BLK, rows[:, :W], 0.0)
            m_ref[...] = m_ref[...] - lax.dot_general(
                later, rows, (((0,), (0,)), ((), ())), precision=HIGHEST, preferred_element_type=jnp.float32
            )

        return carry

    lax.fori_loop(0, W // BLK, step, 0)
    inverse = m_ref[:, W:]
    high = inverse.astype(jnp.bfloat16)
    high_ref[...] = high
    low_ref[...] = (inverse - high.astype(jnp.float32)).astype(jnp.bfloat16)


def factor_inverse(tiles):
    vmem = pl.BlockSpec(memory_space=pltpu.VMEM)
    half = jax.ShapeDtypeStruct((W, W), jnp.bfloat16)
    return pl.pallas_call(
        factor_kernel,
        name="factor",
        in_specs=[vmem],
        out_specs=[vmem, vmem],
        out_shape=[half, half],
        scratch_shapes=[pltpu.VMEM((W, 2 * W), jnp.float32), pltpu.VMEM((BLK, BLK), jnp.float32)],
        compiler_params=pltpu.CompilerParams(vmem_limit_bytes=40 << 20),
    )(tiles)


def split(x):
    high = x.astype(jnp.bfloat16)
    return high, (x - high.astype(jnp.float32)).astype(jnp.bfloat16)


def three_products(x, high, low):
    def product(a, b):
        return lax.dot_general(a, b, (((1,), (1,)), ((), ())), preferred_element_type=jnp.float32)

    x_high, x_low = split(x)
    return (product(x_high, low) + product(x_low, high)) + product(x_high, high)


def panel_kernel(place_ref, *refs):
    rows, cols = refs[:8], refs[8:16]
    inverse_high, inverse_low, panel_ref, high_ref, low_ref, block_ref = refs[16:]
    step = pl.program_id(0)

    def times_inverse(x):
        return three_products(x, inverse_high[...], inverse_low[...])

    @pl.when(step < PR)
    def _():
        for core in range(2):
            for col in range(COLS):
                for x in range(2):
                    source = place_ref[1] ^ (x * 8 + core * 4 + col)
                    start = pl.multiple_of(source * 8, 8)
                    block_ref[pl.ds(start, 8), :] = rows[core * COLS + col][x, 0]
        panel_ref[...] = times_inverse(block_ref[...])

    @pl.when(step >= PR)
    def _():
        for other in range(ROWS):
            start = pl.multiple_of((place_ref[0] ^ other) * 16, 16)
            block_ref[pl.ds(start, 16), :] = cols[other][0]
        value = times_inverse(block_ref[...])
        high_ref[...], low_ref[...] = split(value)


def make_panels(place, rows_raw, cols_raw, inverses):
    def in_rows(i):
        return jnp.minimum(i, PR - 1)

    def in_cols(i):
        return jnp.maximum(i - PR, 0)

    half = jax.ShapeDtypeStruct((PC * BLK, W), jnp.bfloat16)
    return pl.pallas_call(
        panel_kernel,
        name="panels",
        grid_spec=pltpu.PrefetchScalarGridSpec(
            num_scalar_prefetch=1,
            grid=(PR + PC,),
            in_specs=[pl.BlockSpec((2, 1, 8, W), lambda i, p: (0, in_rows(i), 0, 0))] * 8
            + [pl.BlockSpec((1, 16, W), lambda i, p: (in_cols(i), 0, 0))] * ROWS
            + [pl.BlockSpec((W, W), lambda i, p: (0, 0))] * 2,
            out_specs=[
                pl.BlockSpec((BLK, W), lambda i, p: (in_rows(i), 0)),
                pl.BlockSpec((BLK, W), lambda i, p: (in_cols(i), 0)),
                pl.BlockSpec((BLK, W), lambda i, p: (in_cols(i), 0)),
            ],
            scratch_shapes=[pltpu.VMEM((BLK, W), jnp.float32)],
        ),
        out_shape=[jax.ShapeDtypeStruct((PR * BLK, W), jnp.float32), half, half],
        compiler_params=pltpu.CompilerParams(vmem_limit_bytes=32 << 20),
    )(place, *rows_raw, *cols_raw, *inverses)


PAIR = 2


def final_kernel(inv_row_ref, inv_col_ref, lead_ref, *refs):
    recvs = refs[: PAIR * FRONTS]
    parent_ref, panel_ref, high_ref, low_ref = refs[PAIR * FRONTS : PAIR * FRONTS + 4]
    o_ref = refs[-1]
    step = pl.program_id(0)
    panel = panel_ref[:, 0].reshape(PAIR * HALF, W)
    product = three_products(panel, high_ref[...], low_ref[...])
    for part in range(PAIR):
        for b in range(PC):
            span = slice(b * BLK, (b + 1) * BLK)
            total = parent_ref[part, 0, :, span] - product[part * HALF : (part + 1) * HALF, span]
            for front in range(FRONTS):
                r = inv_row_ref[front, step * PAIR + part]
                c = inv_col_ref[front, b]
                ok = jnp.logical_and(r >= 0, c >= 0).astype(jnp.float32)
                total = total + recvs[part * FRONTS + front][jnp.maximum(c, 0)] * ok
            o_ref[part, 0, :, span] = total

    @pl.when(jnp.logical_and(lead_ref[0] == 1, step < WB // PAIR))
    def _():
        o_ref[...] = jnp.zeros_like(o_ref)

    @pl.when(lead_ref[1] == 1)
    def _():
        o_ref[:, :, :, :W] = jnp.zeros((PAIR, 1, HALF, W), jnp.float32)


def finish(place, inv_row, inv_col, lead, recv, parent, panel, high, low, before):
    def recv_map(part, front):
        return lambda i, ir, ic, ld: (
            front * ROWS + jnp.maximum(ir[front, i * PAIR + part], 0),
            0,
            0,
        )

    whole = pl.BlockSpec((PC * BLK, W), lambda a, *_: (0, 0))
    block = pl.BlockSpec((PAIR, 1, HALF, PC * BLK), lambda a, *_: (a, place, 0, 0))
    specs = [
        pl.BlockSpec((COLS, HALF, BLK), recv_map(part, front))
        for part in range(PAIR)
        for front in range(FRONTS)
    ]
    operands = [recv] * len(specs) + [
        parent.reshape(PR, 2, HALF, PC * BLK),
        panel.reshape(PR, 2, HALF, W),
        high,
        low,
    ]
    specs += [block, pl.BlockSpec((PAIR, 1, HALF, W), lambda a, *_: (a, place, 0, 0)), whole, whole]
    aliases = {}
    if before is not None:
        aliases = {3 + len(operands): 0}
        operands.append(before)
        specs.append(pl.BlockSpec(memory_space=pl.ANY))
    return pl.pallas_call(
        final_kernel,
        name="finish",
        grid_spec=pltpu.PrefetchScalarGridSpec(
            num_scalar_prefetch=3, grid=(PR // PAIR,), in_specs=specs, out_specs=block
        ),
        out_shape=jax.ShapeDtypeStruct((PR, 2, HALF, PC * BLK), jnp.float32),
        input_output_aliases=aliases,
        compiler_params=pltpu.CompilerParams(vmem_limit_bytes=40 << 20),
    )(inv_row, inv_col, lead, *operands)


def inverse_places(places, length):
    count = places.shape[1]
    hits = places[:, :, None] == jnp.arange(length, dtype=jnp.int32)
    order = jnp.arange(1, count + 1, dtype=jnp.int32)[None, :, None]
    return jnp.sum(jnp.where(hits, order, 0), axis=1) - 1


def flipped(x, axis, bits):
    size = lax.axis_size(axis)
    return lax.ppermute(x, axis, [(i, i ^ bits) for i in range(size)])


def swap_pairs(flip):
    pairs = []
    for front in range(FRONTS):
        for row in range(ROWS):
            for col in range(COLS):
                group = front * COLS + col
                half = group % 2 if flip == 0 else 1 - group % 2
                to_row, to_group = group // 2, 2 * row + half
                target = (to_group // COLS) * 32 + to_row * COLS + to_group % COLS
                pairs.append((front * 32 + row * COLS + col, target))
    return pairs


def body(parent_entries, child_update, child_map, child_mask):
    row = lax.axis_index("row")
    front = lax.axis_index("front")
    col = lax.axis_index("col")
    group = front * COLS + col
    local = child_update[0]
    window = lax.dynamic_slice(child_mask[0], (row * ROWS, col * GROUPS), (ROWS, GROUPS))

    lead_map = child_map.reshape(FRONTS, COLS, GROUPS)[:, :, 0]
    mine = lax.dynamic_index_in_dim(lead_map, front, 0, keepdims=False)
    p = lax.dynamic_index_in_dim(mine, row // 2, 0, keepdims=False)
    q = lax.dynamic_index_in_dim(mine, col, 0, keepdims=False)
    inside = (row % 2 == 0) & (p < WB) & (q < WB)
    corner_place = jnp.where(inside, p * WB + q, -1)
    holder = (row == 0) & (group == 0)
    info = jnp.stack([corner_place, holder.astype(jnp.int32)]).astype(jnp.int32)

    lead = make_lead(window[:, 0], info, local, parent_entries).reshape(128, 24, BLK)
    lead_recv = lax.all_to_all(lead, ALL, 0, 0, tiled=True)

    first = parent_entries[:, :W].reshape(PR, FRONTS, COLS, 8, W)
    sent = [lax.ppermute(first[:, :, k], "col", [(0, k)]) for k in range(1, COLS)]
    first = jnp.where(col == 0, first[:, :, 0], (sent[0] + sent[1]) + sent[2])

    tiles = jnp.sum(lead_recv[:, 8:], axis=0)
    tiles = jnp.broadcast_to(tiles[None], (128, 16, BLK))
    tiles = lax.all_to_all(tiles, ALL, 0, 0, tiled=True)

    upper, lower = pack(window, local)
    upper, first, tiles = lax.optimization_barrier((upper.reshape(128, HALF, BLK), first, tiles))
    upper_recv = lax.all_to_all(upper, ALL, 0, 0, tiled=True)
    inverses = factor_inverse(tiles)
    first, *inverses = lax.optimization_barrier((first, *inverses))

    sent = [lax.ppermute(first[:, k], "front", [(0, k)]) for k in range(1, FRONTS)]
    first = jnp.where(front == 0, first[:, 0], (sent[0] + sent[1]) + sent[2])

    column = group // 2 + 8 * (group % 2)
    by_row = lax.dynamic_index_in_dim(child_map.reshape(FRONTS, ROWS, 8), row, 2, keepdims=False)
    by_col = lax.dynamic_index_in_dim(
        child_map.reshape(FRONTS, COLS, GROUPS), column, 2, keepdims=False
    )
    inv_row = inverse_places(by_row - row * PR, PR)
    inv_col = inverse_places(by_col - group * PC, PC)
    inv_lead = inverse_places(lead_map, WB)

    slices = assemble_slices(inv_row, inv_lead, lead_recv, first)

    place = jnp.stack([row, group]).astype(jnp.int32)

    pair = jnp.stack([slices, flipped(slices, "front", 2)])
    pair = [pair] + [flipped(pair, "col", bits) for bits in range(1, COLS)]
    rows_raw = pair + [flipped(x, "front", 1) for x in pair]

    even = group % 2 == 0
    one = lax.ppermute(jnp.where(even, slices[:PC], slices[PC:]), ALL, swap_pairs(0))
    two = lax.ppermute(jnp.where(even, slices[PC:], slices[:PC]), ALL, swap_pairs(1))
    mine = jnp.stack([jnp.where(even, one, two), jnp.where(even, two, one)], axis=1)
    mine = mine.reshape(PC, 16, W)
    cols_raw = [mine] + [flipped(mine, "row", bits) for bits in range(1, ROWS)]

    lower, cols_raw, rows_raw = lax.optimization_barrier(
        (lower.reshape(128, HALF, BLK), cols_raw, rows_raw)
    )
    lower_recv = lax.all_to_all(lower, ALL, 0, 0, tiled=True)
    panel, high, low = make_panels(place, rows_raw, cols_raw, inverses)
    lead_flags = jnp.stack([row == 0, group == 0]).astype(jnp.int32)
    args = (parent_entries, panel, high, low)
    schur = finish(0, inv_row, inv_col, lead_flags, upper_recv, *args, None)
    schur = finish(1, inv_row, inv_col, lead_flags, lower_recv, *args, schur)
    return schur.reshape(PR * BLK, PC * BLK), panel


def solution(mesh):
    placed = (P("row", ("front", "col")), P("front", "row", "col"), P(), P("front", None, None))
    return jax.shard_map(
        body,
        mesh=mesh,
        in_specs=placed,
        out_specs=(P("row", ("front", "col")), P("row", None)),
        check_vma=False,
    )
```

```python
import functools

import jax
import jax.numpy as jnp
from jax import lax
from jax.experimental import pallas as pl
from jax.experimental.pallas import tpu as pltpu
from jax.sharding import PartitionSpec as P

W = 512
BLK = 128
HALF = BLK // 2
FRONTS = 4
ROWS = 8
COLS = 4
GROUPS = 16
PR = 12
PC = 6
WB = W // BLK
ALL = ("front", "row", "col")
GRP = ("front", "col")
HIGHEST = lax.Precision.HIGHEST


def group_column(group):
    return group // 2 + 8 * (group % 2)


def pack_kernel(mask_ref, x_ref, upper_ref, lower_ref):
    step = pl.program_id(0)
    for front in range(FRONTS):
        for col in range(COLS):
            v = group_column(front * COLS + col)
            keep = mask_ref[step, v].astype(jnp.float32)
            span = slice(v * BLK, (v + 1) * BLK)
            upper_ref[front, 0, col] = x_ref[:HALF, span] * keep
            lower_ref[front, 0, col] = x_ref[HALF:, span] * keep


def pack(window, local):
    half = jax.ShapeDtypeStruct((FRONTS, ROWS, COLS, HALF, BLK), jnp.float32)
    spec = pl.BlockSpec((FRONTS, 1, COLS, HALF, BLK), lambda i, m: (0, i, 0, 0, 0))
    return pl.pallas_call(
        pack_kernel,
        name="pack",
        grid_spec=pltpu.PrefetchScalarGridSpec(
            num_scalar_prefetch=1,
            grid=(ROWS,),
            in_specs=[pl.BlockSpec((BLK, GROUPS * BLK), lambda i, m: (i, 0))],
            out_specs=[spec, spec],
        ),
        out_shape=[half, half],
        compiler_params=pltpu.CompilerParams(vmem_limit_bytes=32 << 20),
    )(window, local)


def lead_kernel(keep_ref, info_ref, x_ref, parent_ref, o_ref):
    first = (info_ref[1] == 1).astype(jnp.float32)
    for row in range(ROWS):
        keep = keep_ref[row].astype(jnp.float32)
        for group in range(GROUPS):
            front, col = group // COLS, group % COLS
            tile = slice(group * 8, group * 8 + 8)
            o_ref[front, row, col, 0:8] = x_ref[row * BLK + group * 8 : row * BLK + group * 8 + 8, :] * keep
            for j in range(2):
                place = 2 * row + j
                p, q = place // WB, place % WB
                here = keep_ref[0] * (info_ref[0] == place).astype(jnp.int32)
                part = x_ref[tile, :] * here.astype(jnp.float32)
                extra = parent_ref[p * BLK + group * 8 : p * BLK + group * 8 + 8, q * BLK : (q + 1) * BLK]
                o_ref[front, row, col, 8 + 8 * j : 16 + 8 * j] = part + extra * first


def make_lead(keep, info, local, parent):
    return pl.pallas_call(
        lead_kernel,
        name="lead",
        grid_spec=pltpu.PrefetchScalarGridSpec(
            num_scalar_prefetch=2,
            grid=(1,),
            in_specs=[
                pl.BlockSpec((ROWS * BLK, BLK), lambda i, *_: (0, 0)),
                pl.BlockSpec((W, W), lambda i, *_: (0, 0)),
            ],
            out_specs=pl.BlockSpec((FRONTS, ROWS, COLS, 24, BLK), lambda i, *_: (0, 0, 0, 0, 0)),
        ),
        out_shape=jax.ShapeDtypeStruct((FRONTS, ROWS, COLS, 24, BLK), jnp.float32),
    )(keep, info, local, parent)


def slice_kernel(inv_row_ref, inv_lead_ref, recv_ref, parent_ref, o_ref):
    for a in range(PR):
        for q in range(WB):
            total = parent_ref[a, :, q * BLK : (q + 1) * BLK]
            for front in range(FRONTS):
                r = inv_row_ref[front, a]
                c = inv_lead_ref[front, q]
                ok = jnp.logical_and(r >= 0, c >= 0).astype(jnp.float32)
                source = front * 32 + jnp.maximum(r, 0) * COLS + jnp.maximum(c, 0)
                total = total + recv_ref[source, 0:8] * ok
            o_ref[a, :, q * BLK : (q + 1) * BLK] = total


def assemble_slices(inv_row, inv_lead, recv, parent):
    smem = pl.BlockSpec(memory_space=pltpu.SMEM)
    vmem = pl.BlockSpec(memory_space=pltpu.VMEM)
    return pl.pallas_call(
        slice_kernel,
        name="slices",
        in_specs=[smem, smem, vmem, vmem],
        out_specs=vmem,
        out_shape=jax.ShapeDtypeStruct((PR, 8, W), jnp.float32),
    )(inv_row, inv_lead, recv, parent)


KB = 4


def factor_diagonal(get, put):
    groups = BLK // 8
    a = [get(g) for g in range(groups)]
    lanes = lax.broadcasted_iota(jnp.int32, (8, BLK), 1)
    subs = lax.broadcasted_iota(jnp.int32, (8, BLK), 0)
    e = [jnp.where(lanes == subs + 8 * g, 1.0, 0.0).astype(jnp.float32) for g in range(groups)]
    full = (8, BLK)
    for j0 in range(0, BLK, KB):
        g0, i0 = j0 // 8, j0 % 8
        head = [jnp.broadcast_to(a[g0][:, j0 + k : j0 + k + 1], full) for k in range(KB)]
        small = [[None] * KB for _ in range(KB)]
        for i in range(KB):
            for k in range(i + 1):
                small[i][k] = jnp.broadcast_to(head[k][i0 + i : i0 + i + 1, :], full)
        inv = [None] * KB
        low = [[None] * KB for _ in range(KB)]
        for k in range(KB):
            root = lax.rsqrt(small[k][k])
            inv[k] = root * (1.5 - 0.5 * small[k][k] * root * root)
            for i in range(k + 1, KB):
                low[i][k] = small[i][k] * inv[k]
            for i in range(k + 1, KB):
                for m in range(k + 1, i + 1):
                    small[i][m] = small[i][m] - low[i][k] * low[m][k]
        u, w = [], []
        for k in range(KB):
            r = jnp.broadcast_to(a[g0][i0 + k : i0 + k + 1, :], full)
            s = jnp.broadcast_to(e[g0][i0 + k : i0 + k + 1, :], full)
            for m in range(k):
                r = r - low[k][m] * u[m]
                s = s - low[k][m] * w[m]
            u.append(r * inv[k])
            w.append(s * inv[k])
        for g in range(g0, groups):
            if g == g0 and i0 + KB == 8:
                pass
            else:
                mult = []
                for k in range(KB):
                    c = head[k] if g == g0 else jnp.broadcast_to(a[g][:, j0 + k : j0 + k + 1], full)
                    for m in range(k):
                        c = c - mult[m] * low[k][m]
                    mult.append(c * inv[k])
                if g == g0:
                    mult = [jnp.where(subs >= i0 + KB, c, 0.0) for c in mult]
                for k in range(KB):
                    a[g] = a[g] - mult[k] * u[k]
                    e[g] = e[g] - mult[k] * w[k]
            if g == g0:
                for k in range(KB):
                    e[g] = jnp.where(subs == i0 + k, w[k], e[g])
        if i0 + KB == 8:
            put(g0, e[g0])


def factor_kernel(x_ref, high_ref, low_ref, m_ref, d_ref):
    for source in range(FRONTS * ROWS * COLS):
        row = source // COLS % ROWS
        group = source // 32 * COLS + source % COLS
        for j in range(2):
            p, q = (2 * row + j) // WB, (2 * row + j) % WB
            m_ref[p * BLK + group * 8 : p * BLK + group * 8 + 8, q * BLK : (q + 1) * BLK] = x_ref[
                source, 8 * j : 8 * j + 8
            ]
    lanes = lax.broadcasted_iota(jnp.int32, (BLK, BLK), 1)
    subs = lax.broadcasted_iota(jnp.int32, (BLK, BLK), 0)
    eye = jnp.where(lanes == subs, 1.0, 0.0).astype(jnp.float32)
    m_ref[:, W:] = jnp.zeros((W, W), jnp.float32)
    for block in range(W // BLK):
        m_ref[block * BLK : (block + 1) * BLK, W + block * BLK : W + (block + 1) * BLK] = eye

    def step(block, carry):
        base = pl.multiple_of(block * BLK, BLK)

        def get(g):
            return m_ref[pl.ds(pl.multiple_of(base + g * 8, 8), 8), pl.ds(base, BLK)]

        def put(g, value):
            d_ref[g * 8 : (g + 1) * 8, :] = value

        factor_diagonal(get, put)
        rows = jnp.dot(
            d_ref[...], m_ref[pl.ds(base, BLK), :], precision=HIGHEST, preferred_element_type=jnp.float32
        )
        m_ref[pl.ds(base, BLK), :] = rows

        @pl.when(block < W // BLK - 1)
        def _():
            column = lax.broadcasted_iota(jnp.int32, (BLK, W), 1)
            later = jnp.where(column >= base + BLK, rows[:, :W], 0.0)
            m_ref[...] = m_ref[...] - lax.dot_general(
                later, rows, (((0,), (0,)), ((), ())), precision=HIGHEST, preferred_element_type=jnp.float32
            )

        return carry

    lax.fori_loop(0, W // BLK, step, 0)
    inverse = m_ref[:, W:]
    high = inverse.astype(jnp.bfloat16)
    high_ref[...] = high
    low_ref[...] = (inverse - high.astype(jnp.float32)).astype(jnp.bfloat16)


def factor_inverse(tiles):
    vmem = pl.BlockSpec(memory_space=pltpu.VMEM)
    half = jax.ShapeDtypeStruct((W, W), jnp.bfloat16)
    return pl.pallas_call(
        factor_kernel,
        name="factor",
        in_specs=[vmem],
        out_specs=[vmem, vmem],
        out_shape=[half, half],
        scratch_shapes=[pltpu.VMEM((W, 2 * W), jnp.float32), pltpu.VMEM((BLK, BLK), jnp.float32)],
        compiler_params=pltpu.CompilerParams(vmem_limit_bytes=40 << 20),
    )(tiles)


def split(x):
    high = x.astype(jnp.bfloat16)
    return high, (x - high.astype(jnp.float32)).astype(jnp.bfloat16)


def three_products(x, high, low):
    def product(a, b):
        return lax.dot_general(a, b, (((1,), (1,)), ((), ())), preferred_element_type=jnp.float32)

    x_high, x_low = split(x)
    return (product(x_high, low) + product(x_low, high)) + product(x_high, high)


def panel_kernel(place_ref, *refs):
    rows, cols_ref = refs[:8], refs[8]
    inverse_high, inverse_low, panel_ref, high_ref, low_ref, block_ref = refs[9:]
    step = pl.program_id(0)

    def times_inverse(x):
        return three_products(x, inverse_high[...], inverse_low[...])

    @pl.when(step < PR)
    def _():
        for core in range(2):
            for col in range(COLS):
                for x in range(2):
                    source = place_ref[1] ^ (x * 8 + core * 4 + col)
                    start = pl.multiple_of(source * 8, 8)
                    block_ref[pl.ds(start, 8), :] = rows[core * COLS + col][x, 0]
        panel_ref[...] = times_inverse(block_ref[...])

    @pl.when(step >= PR)
    def _():
        value = times_inverse(cols_ref[:, 0].reshape(BLK, W))
        high_ref[...], low_ref[...] = split(value)


def make_panels(place, rows_raw, cols_raw, inverses):
    def in_rows(i):
        return jnp.minimum(i, PR - 1)

    def in_cols(i):
        return jnp.maximum(i - PR, 0)

    half = jax.ShapeDtypeStruct((PC * BLK, W), jnp.bfloat16)
    return pl.pallas_call(
        panel_kernel,
        name="panels",
        grid_spec=pltpu.PrefetchScalarGridSpec(
            num_scalar_prefetch=1,
            grid=(PR + PC,),
            in_specs=[pl.BlockSpec((2, 1, 8, W), lambda i, p: (0, in_rows(i), 0, 0))] * 8
            + [pl.BlockSpec((ROWS, 1, 16, W), lambda i, p: (0, in_cols(i), 0, 0))]
            + [pl.BlockSpec((W, W), lambda i, p: (0, 0))] * 2,
            out_specs=[
                pl.BlockSpec((BLK, W), lambda i, p: (in_rows(i), 0)),
                pl.BlockSpec((BLK, W), lambda i, p: (in_cols(i), 0)),
                pl.BlockSpec((BLK, W), lambda i, p: (in_cols(i), 0)),
            ],
            scratch_shapes=[pltpu.VMEM((BLK, W), jnp.float32)],
        ),
        out_shape=[jax.ShapeDtypeStruct((PR * BLK, W), jnp.float32), half, half],
        compiler_params=pltpu.CompilerParams(vmem_limit_bytes=32 << 20),
    )(place, *rows_raw, cols_raw, *inverses)


PAIR = 4


def final_kernel(inv_row_ref, inv_col_ref, lead_ref, *refs):
    recvs = refs[: PAIR * FRONTS]
    parent_ref, panel_ref, high_ref, low_ref = refs[PAIR * FRONTS : PAIR * FRONTS + 4]
    o_ref = refs[-1]
    step = pl.program_id(0)
    panel = panel_ref[:, 0].reshape(PAIR * HALF, W)
    product = three_products(panel, high_ref[...], low_ref[...])
    for part in range(PAIR):
        for b in range(PC):
            span = slice(b * BLK, (b + 1) * BLK)
            total = parent_ref[part, 0, :, span] - product[part * HALF : (part + 1) * HALF, span]
            for front in range(FRONTS):
                r = inv_row_ref[front, step * PAIR + part]
                c = inv_col_ref[front, b]
                ok = jnp.logical_and(r >= 0, c >= 0).astype(jnp.float32)
                total = total + recvs[part * FRONTS + front][jnp.maximum(c, 0)] * ok
            o_ref[part, 0, :, span] = total

    @pl.when(jnp.logical_and(lead_ref[0] == 1, step < WB // PAIR))
    def _():
        o_ref[...] = jnp.zeros_like(o_ref)

    @pl.when(lead_ref[1] == 1)
    def _():
        o_ref[:, :, :, :W] = jnp.zeros((PAIR, 1, HALF, W), jnp.float32)


def finish(place, inv_row, inv_col, lead, recv, parent, panel, high, low, before):
    def recv_map(part, front):
        return lambda i, ir, ic, ld: (
            front * ROWS + jnp.maximum(ir[front, i * PAIR + part], 0),
            0,
            0,
        )

    whole = pl.BlockSpec((PC * BLK, W), lambda a, *_: (0, 0))
    block = pl.BlockSpec((PAIR, 1, HALF, PC * BLK), lambda a, *_: (a, place, 0, 0))
    specs = [
        pl.BlockSpec((COLS, HALF, BLK), recv_map(part, front))
        for part in range(PAIR)
        for front in range(FRONTS)
    ]
    operands = [recv] * len(specs) + [
        parent.reshape(PR, 2, HALF, PC * BLK),
        panel.reshape(PR, 2, HALF, W),
        high,
        low,
    ]
    specs += [block, pl.BlockSpec((PAIR, 1, HALF, W), lambda a, *_: (a, place, 0, 0)), whole, whole]
    aliases = {}
    if before is not None:
        aliases = {3 + len(operands): 0}
        operands.append(before)
        specs.append(pl.BlockSpec(memory_space=pl.ANY))
    return pl.pallas_call(
        final_kernel,
        name="finish",
        grid_spec=pltpu.PrefetchScalarGridSpec(
            num_scalar_prefetch=3, grid=(PR // PAIR,), in_specs=specs, out_specs=block
        ),
        out_shape=jax.ShapeDtypeStruct((PR, 2, HALF, PC * BLK), jnp.float32),
        input_output_aliases=aliases,
        compiler_params=pltpu.CompilerParams(vmem_limit_bytes=56 << 20),
    )(inv_row, inv_col, lead, *operands)


def inverse_places(places, length):
    count = places.shape[1]
    hits = places[:, :, None] == jnp.arange(length, dtype=jnp.int32)
    order = jnp.arange(1, count + 1, dtype=jnp.int32)[None, :, None]
    return jnp.sum(jnp.where(hits, order, 0), axis=1) - 1


def flipped(x, axis, bits):
    size = lax.axis_size(axis)
    return lax.ppermute(x, axis, [(i, i ^ bits) for i in range(size)])


def swap_pairs(flip):
    pairs = []
    for front in range(FRONTS):
        for row in range(ROWS):
            for col in range(COLS):
                group = front * COLS + col
                half = group % 2 if flip == 0 else 1 - group % 2
                to_row, to_group = group // 2, 2 * row + half
                target = (to_group // COLS) * 32 + to_row * COLS + to_group % COLS
                pairs.append((front * 32 + row * COLS + col, target))
    return pairs


def body(parent_entries, child_update, child_map, child_mask):
    row = lax.axis_index("row")
    front = lax.axis_index("front")
    col = lax.axis_index("col")
    group = front * COLS + col
    local = child_update[0]
    window = lax.dynamic_slice(child_mask[0], (row * ROWS, col * GROUPS), (ROWS, GROUPS))

    lead_map = child_map.reshape(FRONTS, COLS, GROUPS)[:, :, 0]
    mine = lax.dynamic_index_in_dim(lead_map, front, 0, keepdims=False)
    p = lax.dynamic_index_in_dim(mine, row // 2, 0, keepdims=False)
    q = lax.dynamic_index_in_dim(mine, col, 0, keepdims=False)
    inside = (row % 2 == 0) & (p < WB) & (q < WB)
    corner_place = jnp.where(inside, p * WB + q, -1)
    holder = (row == 0) & (group == 0)
    info = jnp.stack([corner_place, holder.astype(jnp.int32)]).astype(jnp.int32)

    lead = make_lead(window[:, 0], info, local, parent_entries).reshape(128, 24, BLK)

    first = parent_entries[:, :W].reshape(PR, FRONTS, COLS, 8, W)
    sent = [lax.ppermute(first[:, :, k], "col", [(0, k)]) for k in range(1, COLS)]
    first = first[:, :, 0]

    upper, lower = pack(window, local)
    upper, sent[0], sent[1], sent[2] = lax.optimization_barrier((upper, *sent))
    upper_recv = lax.all_to_all(upper.reshape(128, HALF, BLK), ALL, 0, 0, tiled=True)
    first = jnp.where(col == 0, first, (sent[0] + sent[1]) + sent[2])

    lead, upper_recv = lax.optimization_barrier((lead, upper_recv))
    lead_recv = lax.all_to_all(lead, ALL, 0, 0, tiled=True)

    tiles = jnp.sum(lead_recv[:, 8:], axis=0)
    tiles = jnp.broadcast_to(tiles[None], (128, 16, BLK))
    tiles = lax.all_to_all(tiles, ALL, 0, 0, tiled=True)

    sent = [lax.ppermute(first[:, k], "front", [(0, k)]) for k in range(1, FRONTS)]
    first = jnp.where(front == 0, first[:, 0], (sent[0] + sent[1]) + sent[2])

    column = group // 2 + 8 * (group % 2)
    by_row = lax.dynamic_index_in_dim(child_map.reshape(FRONTS, ROWS, 8), row, 2, keepdims=False)
    by_col = lax.dynamic_index_in_dim(
        child_map.reshape(FRONTS, COLS, GROUPS), column, 2, keepdims=False
    )
    inv_row = inverse_places(by_row - row * PR, PR)
    inv_col = inverse_places(by_col - group * PC, PC)
    inv_lead = inverse_places(lead_map, WB)

    slices = assemble_slices(inv_row, inv_lead, lead_recv, first)

    place = jnp.stack([row, group]).astype(jnp.int32)

    pair = jnp.stack([slices, flipped(slices, "front", 2)])
    pair = [pair] + [flipped(pair, "col", bits) for bits in range(1, COLS)]
    rows_raw = pair + [flipped(x, "front", 1) for x in pair]

    even = group % 2 == 0
    one = lax.ppermute(jnp.where(even, slices[:PC], slices[PC:]), ALL, swap_pairs(0))
    two = lax.ppermute(jnp.where(even, slices[PC:], slices[:PC]), ALL, swap_pairs(1))
    mine = jnp.stack([jnp.where(even, one, two), jnp.where(even, two, one)], axis=1)
    mine = mine.reshape(PC, 16, W)
    mine = jnp.broadcast_to(mine.reshape(1, PC * 16, W), (ROWS, PC * 16, W))
    cols_raw = lax.all_to_all(mine, "row", 0, 0, tiled=True).reshape(ROWS, PC, 16, W)

    lower, tiles, cols_raw, rows_raw = lax.optimization_barrier(
        (lower.reshape(128, HALF, BLK), tiles, cols_raw, rows_raw)
    )
    inverses = factor_inverse(tiles)
    lower_recv = lax.all_to_all(lower, ALL, 0, 0, tiled=True)
    panel, high, low = make_panels(place, rows_raw, cols_raw, inverses)
    lead_flags = jnp.stack([row == 0, group == 0]).astype(jnp.int32)
    args = (parent_entries, panel, high, low)
    schur = finish(0, inv_row, inv_col, lead_flags, upper_recv, *args, None)
    schur = finish(1, inv_row, inv_col, lead_flags, lower_recv, *args, schur)
    return schur.reshape(PR * BLK, PC * BLK), panel


def solution(mesh):
    placed = (P("row", ("front", "col")), P("front", "row", "col"), P(), P("front", None, None))
    return jax.shard_map(
        body,
        mesh=mesh,
        in_specs=placed,
        out_specs=(P("row", ("front", "col")), P("row", None)),
        check_vma=False,
    )
```

```python
import functools

import jax
import jax.numpy as jnp
from jax import lax
from jax.experimental import pallas as pl
from jax.experimental.pallas import tpu as pltpu
from jax.sharding import PartitionSpec as P

W = 512
BLK = 128
HALF = BLK // 2
FRONTS = 4
ROWS = 8
COLS = 4
GROUPS = 16
PR = 12
PC = 6
WB = W // BLK
ALL = ("front", "row", "col")
GRP = ("front", "col")
HIGHEST = lax.Precision.HIGHEST


def group_column(group):
    return group // 2 + 8 * (group % 2)


def pack_kernel(mask_ref, x_ref, upper_ref, lower_ref):
    step = pl.program_id(0)
    for front in range(FRONTS):
        for col in range(COLS):
            v = group_column(front * COLS + col)
            keep = mask_ref[step, v].astype(jnp.float32)
            span = slice(v * BLK, (v + 1) * BLK)
            upper_ref[front, 0, col] = x_ref[:HALF, span] * keep
            lower_ref[front, 0, col] = x_ref[HALF:, span] * keep


def pack(window, local):
    half = jax.ShapeDtypeStruct((FRONTS, ROWS, COLS, HALF, BLK), jnp.float32)
    spec = pl.BlockSpec((FRONTS, 1, COLS, HALF, BLK), lambda i, m: (0, i, 0, 0, 0))
    return pl.pallas_call(
        pack_kernel,
        name="pack",
        grid_spec=pltpu.PrefetchScalarGridSpec(
            num_scalar_prefetch=1,
            grid=(ROWS,),
            in_specs=[pl.BlockSpec((BLK, GROUPS * BLK), lambda i, m: (i, 0))],
            out_specs=[spec, spec],
        ),
        out_shape=[half, half],
        compiler_params=pltpu.CompilerParams(vmem_limit_bytes=32 << 20),
    )(window, local)


def lead_kernel(keep_ref, info_ref, x_ref, parent_ref, o_ref):
    first = (info_ref[1] == 1).astype(jnp.float32)
    for row in range(ROWS):
        keep = keep_ref[row].astype(jnp.float32)
        for group in range(GROUPS):
            front, col = group // COLS, group % COLS
            tile = slice(group * 8, group * 8 + 8)
            o_ref[front, row, col, 0:8] = x_ref[row * BLK + group * 8 : row * BLK + group * 8 + 8, :] * keep
            for j in range(2):
                place = 2 * row + j
                p, q = place // WB, place % WB
                here = keep_ref[0] * (info_ref[0] == place).astype(jnp.int32)
                part = x_ref[tile, :] * here.astype(jnp.float32)
                extra = parent_ref[p * BLK + group * 8 : p * BLK + group * 8 + 8, q * BLK : (q + 1) * BLK]
                o_ref[front, row, col, 8 + 8 * j : 16 + 8 * j] = part + extra * first


def make_lead(keep, info, local, parent):
    return pl.pallas_call(
        lead_kernel,
        name="lead",
        grid_spec=pltpu.PrefetchScalarGridSpec(
            num_scalar_prefetch=2,
            grid=(1,),
            in_specs=[
                pl.BlockSpec((ROWS * BLK, BLK), lambda i, *_: (0, 0)),
                pl.BlockSpec((W, W), lambda i, *_: (0, 0)),
            ],
            out_specs=pl.BlockSpec((FRONTS, ROWS, COLS, 24, BLK), lambda i, *_: (0, 0, 0, 0, 0)),
        ),
        out_shape=jax.ShapeDtypeStruct((FRONTS, ROWS, COLS, 24, BLK), jnp.float32),
    )(keep, info, local, parent)


def slice_kernel(inv_row_ref, inv_lead_ref, recv_ref, parent_ref, o_ref):
    for a in range(PR):
        for q in range(WB):
            total = parent_ref[a, :, q * BLK : (q + 1) * BLK]
            for front in range(FRONTS):
                r = inv_row_ref[front, a]
                c = inv_lead_ref[front, q]
                ok = jnp.logical_and(r >= 0, c >= 0).astype(jnp.float32)
                source = front * 32 + jnp.maximum(r, 0) * COLS + jnp.maximum(c, 0)
                total = total + recv_ref[source, 0:8] * ok
            o_ref[a, :, q * BLK : (q + 1) * BLK] = total


def assemble_slices(inv_row, inv_lead, recv, parent):
    smem = pl.BlockSpec(memory_space=pltpu.SMEM)
    vmem = pl.BlockSpec(memory_space=pltpu.VMEM)
    return pl.pallas_call(
        slice_kernel,
        name="slices",
        in_specs=[smem, smem, vmem, vmem],
        out_specs=vmem,
        out_shape=jax.ShapeDtypeStruct((PR, 8, W), jnp.float32),
    )(inv_row, inv_lead, recv, parent)


KB = 4


def factor_diagonal(get, put):
    groups = BLK // 8
    a = [get(g) for g in range(groups)]
    lanes = lax.broadcasted_iota(jnp.int32, (8, BLK), 1)
    subs = lax.broadcasted_iota(jnp.int32, (8, BLK), 0)
    e = [jnp.where(lanes == subs + 8 * g, 1.0, 0.0).astype(jnp.float32) for g in range(groups)]
    full = (8, BLK)
    for j0 in range(0, BLK, KB):
        g0, i0 = j0 // 8, j0 % 8
        head = [jnp.broadcast_to(a[g0][:, j0 + k : j0 + k + 1], full) for k in range(KB)]
        small = [[None] * KB for _ in range(KB)]
        for i in range(KB):
            for k in range(i + 1):
                small[i][k] = jnp.broadcast_to(head[k][i0 + i : i0 + i + 1, :], full)
        inv = [None] * KB
        low = [[None] * KB for _ in range(KB)]
        for k in range(KB):
            root = lax.rsqrt(small[k][k])
            inv[k] = root * (1.5 - 0.5 * small[k][k] * root * root)
            for i in range(k + 1, KB):
                low[i][k] = small[i][k] * inv[k]
            for i in range(k + 1, KB):
                for m in range(k + 1, i + 1):
                    small[i][m] = small[i][m] - low[i][k] * low[m][k]
        u, w = [], []
        for k in range(KB):
            r = jnp.broadcast_to(a[g0][i0 + k : i0 + k + 1, :], full)
            s = jnp.broadcast_to(e[g0][i0 + k : i0 + k + 1, :], full)
            for m in range(k):
                r = r - low[k][m] * u[m]
                s = s - low[k][m] * w[m]
            u.append(r * inv[k])
            w.append(s * inv[k])
        for g in range(g0, groups):
            if g == g0 and i0 + KB == 8:
                pass
            else:
                mult = []
                for k in range(KB):
                    c = head[k] if g == g0 else jnp.broadcast_to(a[g][:, j0 + k : j0 + k + 1], full)
                    for m in range(k):
                        c = c - mult[m] * low[k][m]
                    mult.append(c * inv[k])
                if g == g0:
                    mult = [jnp.where(subs >= i0 + KB, c, 0.0) for c in mult]
                for k in range(KB):
                    a[g] = a[g] - mult[k] * u[k]
                    e[g] = e[g] - mult[k] * w[k]
            if g == g0:
                for k in range(KB):
                    e[g] = jnp.where(subs == i0 + k, w[k], e[g])
        if i0 + KB == 8:
            put(g0, e[g0])


def factor_kernel(x_ref, high_ref, low_ref, m_ref, d_ref):
    for source in range(FRONTS * ROWS * COLS):
        row = source // COLS % ROWS
        group = source // 32 * COLS + source % COLS
        for j in range(2):
            p, q = (2 * row + j) // WB, (2 * row + j) % WB
            m_ref[p * BLK + group * 8 : p * BLK + group * 8 + 8, q * BLK : (q + 1) * BLK] = x_ref[
                source, 8 * j : 8 * j + 8
            ]
    lanes = lax.broadcasted_iota(jnp.int32, (BLK, BLK), 1)
    subs = lax.broadcasted_iota(jnp.int32, (BLK, BLK), 0)
    eye = jnp.where(lanes == subs, 1.0, 0.0).astype(jnp.float32)
    m_ref[:, W:] = jnp.zeros((W, W), jnp.float32)
    for block in range(W // BLK):
        m_ref[block * BLK : (block + 1) * BLK, W + block * BLK : W + (block + 1) * BLK] = eye

    def step(block, carry):
        base = pl.multiple_of(block * BLK, BLK)

        def get(g):
            return m_ref[pl.ds(pl.multiple_of(base + g * 8, 8), 8), pl.ds(base, BLK)]

        def put(g, value):
            d_ref[g * 8 : (g + 1) * 8, :] = value

        factor_diagonal(get, put)
        rows = jnp.dot(
            d_ref[...], m_ref[pl.ds(base, BLK), :], precision=HIGHEST, preferred_element_type=jnp.float32
        )
        m_ref[pl.ds(base, BLK), :] = rows

        @pl.when(block < W // BLK - 1)
        def _():
            column = lax.broadcasted_iota(jnp.int32, (BLK, W), 1)
            later = jnp.where(column >= base + BLK, rows[:, :W], 0.0)
            m_ref[...] = m_ref[...] - lax.dot_general(
                later, rows, (((0,), (0,)), ((), ())), precision=HIGHEST, preferred_element_type=jnp.float32
            )

        return carry

    lax.fori_loop(0, W // BLK, step, 0)
    inverse = m_ref[:, W:]
    high = inverse.astype(jnp.bfloat16)
    high_ref[...] = high
    low_ref[...] = (inverse - high.astype(jnp.float32)).astype(jnp.bfloat16)


def factor_inverse(tiles):
    vmem = pl.BlockSpec(memory_space=pltpu.VMEM)
    half = jax.ShapeDtypeStruct((W, W), jnp.bfloat16)
    return pl.pallas_call(
        factor_kernel,
        name="factor",
        in_specs=[vmem],
        out_specs=[vmem, vmem],
        out_shape=[half, half],
        scratch_shapes=[pltpu.VMEM((W, 2 * W), jnp.float32), pltpu.VMEM((BLK, BLK), jnp.float32)],
        compiler_params=pltpu.CompilerParams(vmem_limit_bytes=40 << 20),
    )(tiles)


def split(x):
    high = x.astype(jnp.bfloat16)
    return high, (x - high.astype(jnp.float32)).astype(jnp.bfloat16)


def three_products(x, high, low):
    def product(a, b):
        return lax.dot_general(a, b, (((1,), (1,)), ((), ())), preferred_element_type=jnp.float32)

    x_high, x_low = split(x)
    return (product(x_high, low) + product(x_low, high)) + product(x_high, high)


def panel_kernel(place_ref, *refs):
    rows, cols_ref = refs[:8], refs[8]
    inverse_high, inverse_low, panel_ref, high_ref, low_ref, block_ref = refs[9:]
    step = pl.program_id(0)

    def times_inverse(x):
        return three_products(x, inverse_high[...], inverse_low[...])

    @pl.when(step < PR)
    def _():
        for core in range(2):
            for col in range(COLS):
                for x in range(2):
                    source = place_ref[1] ^ (x * 8 + core * 4 + col)
                    start = pl.multiple_of(source * 8, 8)
                    block_ref[pl.ds(start, 8), :] = rows[core * COLS + col][x, 0]
        panel_ref[...] = times_inverse(block_ref[...])

    @pl.when(step >= PR)
    def _():
        value = times_inverse(cols_ref[:, 0].reshape(BLK, W))
        high_ref[...], low_ref[...] = split(value)


def make_panels(place, rows_raw, cols_raw, inverses):
    def in_rows(i):
        return jnp.minimum(i, PR - 1)

    def in_cols(i):
        return jnp.maximum(i - PR, 0)

    half = jax.ShapeDtypeStruct((PC * BLK, W), jnp.bfloat16)
    return pl.pallas_call(
        panel_kernel,
        name="panels",
        grid_spec=pltpu.PrefetchScalarGridSpec(
            num_scalar_prefetch=1,
            grid=(PR + PC,),
            in_specs=[pl.BlockSpec((2, 1, 8, W), lambda i, p: (0, in_rows(i), 0, 0))] * 8
            + [pl.BlockSpec((ROWS, 1, 16, W), lambda i, p: (0, in_cols(i), 0, 0))]
            + [pl.BlockSpec((W, W), lambda i, p: (0, 0))] * 2,
            out_specs=[
                pl.BlockSpec((BLK, W), lambda i, p: (in_rows(i), 0)),
                pl.BlockSpec((BLK, W), lambda i, p: (in_cols(i), 0)),
                pl.BlockSpec((BLK, W), lambda i, p: (in_cols(i), 0)),
            ],
            scratch_shapes=[pltpu.VMEM((BLK, W), jnp.float32)],
        ),
        out_shape=[jax.ShapeDtypeStruct((PR * BLK, W), jnp.float32), half, half],
        compiler_params=pltpu.CompilerParams(vmem_limit_bytes=32 << 20),
    )(place, *rows_raw, cols_raw, *inverses)


PAIR = 4


def final_kernel(inv_row_ref, inv_col_ref, lead_ref, *refs):
    recvs = refs[: PAIR * FRONTS]
    parent_ref, panel_ref, high_ref, low_ref = refs[PAIR * FRONTS : PAIR * FRONTS + 4]
    o_ref = refs[-1]
    step = pl.program_id(0)
    panel = panel_ref[:, 0].reshape(PAIR * HALF, W)
    product = three_products(panel, high_ref[...], low_ref[...])
    for part in range(PAIR):
        for b in range(PC):
            span = slice(b * BLK, (b + 1) * BLK)
            total = parent_ref[part, 0, :, span] - product[part * HALF : (part + 1) * HALF, span]
            for front in range(FRONTS):
                r = inv_row_ref[front, step * PAIR + part]
                c = inv_col_ref[front, b]
                ok = jnp.logical_and(r >= 0, c >= 0).astype(jnp.float32)
                total = total + recvs[part * FRONTS + front][jnp.maximum(c, 0)] * ok
            o_ref[part, 0, :, span] = total

    @pl.when(jnp.logical_and(lead_ref[0] == 1, step < WB // PAIR))
    def _():
        o_ref[...] = jnp.zeros_like(o_ref)

    @pl.when(lead_ref[1] == 1)
    def _():
        o_ref[:, :, :, :W] = jnp.zeros((PAIR, 1, HALF, W), jnp.float32)


def finish(place, inv_row, inv_col, lead, recv, parent, panel, high, low, before):
    def recv_map(part, front):
        return lambda i, ir, ic, ld: (
            front * ROWS + jnp.maximum(ir[front, i * PAIR + part], 0),
            0,
            0,
        )

    whole = pl.BlockSpec((PC * BLK, W), lambda a, *_: (0, 0))
    block = pl.BlockSpec((PAIR, 1, HALF, PC * BLK), lambda a, *_: (a, place, 0, 0))
    specs = [
        pl.BlockSpec((COLS, HALF, BLK), recv_map(part, front))
        for part in range(PAIR)
        for front in range(FRONTS)
    ]
    operands = [recv] * len(specs) + [
        parent.reshape(PR, 2, HALF, PC * BLK),
        panel.reshape(PR, 2, HALF, W),
        high,
        low,
    ]
    specs += [block, pl.BlockSpec((PAIR, 1, HALF, W), lambda a, *_: (a, place, 0, 0)), whole, whole]
    aliases = {}
    if before is not None:
        aliases = {3 + len(operands): 0}
        operands.append(before)
        specs.append(pl.BlockSpec(memory_space=pl.ANY))
    return pl.pallas_call(
        final_kernel,
        name="finish",
        grid_spec=pltpu.PrefetchScalarGridSpec(
            num_scalar_prefetch=3, grid=(PR // PAIR,), in_specs=specs, out_specs=block
        ),
        out_shape=jax.ShapeDtypeStruct((PR, 2, HALF, PC * BLK), jnp.float32),
        input_output_aliases=aliases,
        compiler_params=pltpu.CompilerParams(vmem_limit_bytes=56 << 20),
    )(inv_row, inv_col, lead, *operands)


def inverse_places(places, length):
    count = places.shape[1]
    hits = places[:, :, None] == jnp.arange(length, dtype=jnp.int32)
    order = jnp.arange(1, count + 1, dtype=jnp.int32)[None, :, None]
    return jnp.sum(jnp.where(hits, order, 0), axis=1) - 1


def flipped(x, axis, bits):
    size = lax.axis_size(axis)
    return lax.ppermute(x, axis, [(i, i ^ bits) for i in range(size)])


def swap_pairs(flip):
    pairs = []
    for front in range(FRONTS):
        for row in range(ROWS):
            for col in range(COLS):
                group = front * COLS + col
                half = group % 2 if flip == 0 else 1 - group % 2
                to_row, to_group = group // 2, 2 * row + half
                target = (to_group // COLS) * 32 + to_row * COLS + to_group % COLS
                pairs.append((front * 32 + row * COLS + col, target))
    return pairs


def body(parent_entries, child_update, child_map, child_mask):
    row = lax.axis_index("row")
    front = lax.axis_index("front")
    col = lax.axis_index("col")
    group = front * COLS + col
    local = child_update[0]
    window = lax.dynamic_slice(child_mask[0], (row * ROWS, col * GROUPS), (ROWS, GROUPS))

    lead_map = child_map.reshape(FRONTS, COLS, GROUPS)[:, :, 0]
    mine = lax.dynamic_index_in_dim(lead_map, front, 0, keepdims=False)
    p = lax.dynamic_index_in_dim(mine, row // 2, 0, keepdims=False)
    q = lax.dynamic_index_in_dim(mine, col, 0, keepdims=False)
    inside = (row % 2 == 0) & (p < WB) & (q < WB)
    corner_place = jnp.where(inside, p * WB + q, -1)
    holder = (row == 0) & (group == 0)
    info = jnp.stack([corner_place, holder.astype(jnp.int32)]).astype(jnp.int32)

    lead = make_lead(window[:, 0], info, local, parent_entries).reshape(128, 24, BLK)
    lead_recv = lax.all_to_all(lead, ALL, 0, 0, tiled=True)

    first = parent_entries[:, :W].reshape(PR, FRONTS, COLS, 8, W)
    sent = [lax.ppermute(first[:, :, k], "col", [(0, k)]) for k in range(1, COLS)]
    first = jnp.where(col == 0, first[:, :, 0], (sent[0] + sent[1]) + sent[2])

    tiles = jnp.sum(lead_recv[:, 8:], axis=0)
    tiles = jnp.broadcast_to(tiles[None], (128, 16, BLK))
    tiles = lax.all_to_all(tiles, ALL, 0, 0, tiled=True)

    upper, lower = pack(window, local)
    upper, first, tiles = lax.optimization_barrier((upper.reshape(128, HALF, BLK), first, tiles))
    upper_recv = lax.all_to_all(upper, ALL, 0, 0, tiled=True)
    inverses = factor_inverse(tiles)
    first, *inverses = lax.optimization_barrier((first, *inverses))

    sent = [lax.ppermute(first[:, k], "front", [(0, k)]) for k in range(1, FRONTS)]
    first = jnp.where(front == 0, first[:, 0], (sent[0] + sent[1]) + sent[2])

    column = group // 2 + 8 * (group % 2)
    by_row = lax.dynamic_index_in_dim(child_map.reshape(FRONTS, ROWS, 8), row, 2, keepdims=False)
    by_col = lax.dynamic_index_in_dim(
        child_map.reshape(FRONTS, COLS, GROUPS), column, 2, keepdims=False
    )
    inv_row = inverse_places(by_row - row * PR, PR)
    inv_col = inverse_places(by_col - group * PC, PC)
    inv_lead = inverse_places(lead_map, WB)

    slices = assemble_slices(inv_row, inv_lead, lead_recv, first)

    place = jnp.stack([row, group]).astype(jnp.int32)

    even = group % 2 == 0
    one = lax.ppermute(jnp.where(even, slices[:PC], slices[PC:]), ALL, swap_pairs(0))
    two = lax.ppermute(jnp.where(even, slices[PC:], slices[:PC]), ALL, swap_pairs(1))
    mine = jnp.stack([jnp.where(even, one, two), jnp.where(even, two, one)], axis=1)
    mine = mine.reshape(PC, 16, W)
    pair = jnp.stack([slices, flipped(slices, "front", 2)])
    pair = [pair] + [flipped(pair, "col", bits) for bits in range(1, COLS)]
    mine, *pair = lax.optimization_barrier((mine, *pair))
    rows_raw = pair + [flipped(x, "front", 1) for x in pair]

    mine, upper_recv = lax.optimization_barrier((mine, upper_recv))
    mine = jnp.broadcast_to(mine.reshape(1, PC * 16, W), (ROWS, PC * 16, W))
    cols_raw = lax.all_to_all(mine, "row", 0, 0, tiled=True).reshape(ROWS, PC, 16, W)

    lower, cols_raw, rows_raw = lax.optimization_barrier(
        (lower.reshape(128, HALF, BLK), cols_raw, rows_raw)
    )
    lower_recv = lax.all_to_all(lower, ALL, 0, 0, tiled=True)
    panel, high, low = make_panels(place, rows_raw, cols_raw, inverses)
    lead_flags = jnp.stack([row == 0, group == 0]).astype(jnp.int32)
    args = (parent_entries, panel, high, low)
    schur = finish(0, inv_row, inv_col, lead_flags, upper_recv, *args, None)
    schur = finish(1, inv_row, inv_col, lead_flags, lower_recv, *args, schur)
    return schur.reshape(PR * BLK, PC * BLK), panel


def solution(mesh):
    placed = (P("row", ("front", "col")), P("front", "row", "col"), P(), P("front", None, None))
    return jax.shard_map(
        body,
        mesh=mesh,
        in_specs=placed,
        out_specs=(P("row", ("front", "col")), P("row", None)),
        check_vma=False,
    )
```

```python
import functools

import jax
import jax.numpy as jnp
from jax import lax
from jax.experimental import pallas as pl
from jax.experimental.pallas import tpu as pltpu
from jax.sharding import PartitionSpec as P

W = 512
BLK = 128
HALF = BLK // 2
FRONTS = 4
ROWS = 8
COLS = 4
GROUPS = 16
PR = 12
PC = 6
WB = W // BLK
ALL = ("front", "row", "col")
GRP = ("front", "col")
HIGHEST = lax.Precision.HIGHEST


def group_column(group):
    return group // 2 + 8 * (group % 2)


def pack_kernel(mask_ref, x_ref, upper_ref, lower_ref):
    step = pl.program_id(0)
    for front in range(FRONTS):
        for col in range(COLS):
            v = group_column(front * COLS + col)
            keep = mask_ref[step, v].astype(jnp.float32)
            span = slice(v * BLK, (v + 1) * BLK)
            upper_ref[front, 0, col] = x_ref[:HALF, span] * keep
            lower_ref[front, 0, col] = x_ref[HALF:, span] * keep


def pack(window, local):
    half = jax.ShapeDtypeStruct((FRONTS, ROWS, COLS, HALF, BLK), jnp.float32)
    spec = pl.BlockSpec((FRONTS, 1, COLS, HALF, BLK), lambda i, m: (0, i, 0, 0, 0))
    return pl.pallas_call(
        pack_kernel,
        name="pack",
        grid_spec=pltpu.PrefetchScalarGridSpec(
            num_scalar_prefetch=1,
            grid=(ROWS,),
            in_specs=[pl.BlockSpec((BLK, GROUPS * BLK), lambda i, m: (i, 0))],
            out_specs=[spec, spec],
        ),
        out_shape=[half, half],
        compiler_params=pltpu.CompilerParams(vmem_limit_bytes=32 << 20),
    )(window, local)


def lead_kernel(keep_ref, info_ref, x_ref, parent_ref, o_ref):
    first = (info_ref[1] == 1).astype(jnp.float32)
    for row in range(ROWS):
        keep = keep_ref[row].astype(jnp.float32)
        for group in range(GROUPS):
            front, col = group // COLS, group % COLS
            tile = slice(group * 8, group * 8 + 8)
            o_ref[front, row, col, 0:8] = x_ref[row * BLK + group * 8 : row * BLK + group * 8 + 8, :] * keep
            for j in range(2):
                place = 2 * row + j
                p, q = place // WB, place % WB
                here = keep_ref[0] * (info_ref[0] == place).astype(jnp.int32)
                part = x_ref[tile, :] * here.astype(jnp.float32)
                extra = parent_ref[p * BLK + group * 8 : p * BLK + group * 8 + 8, q * BLK : (q + 1) * BLK]
                o_ref[front, row, col, 8 + 8 * j : 16 + 8 * j] = part + extra * first


def make_lead(keep, info, local, parent):
    return pl.pallas_call(
        lead_kernel,
        name="lead",
        grid_spec=pltpu.PrefetchScalarGridSpec(
            num_scalar_prefetch=2,
            grid=(1,),
            in_specs=[
                pl.BlockSpec((ROWS * BLK, BLK), lambda i, *_: (0, 0)),
                pl.BlockSpec((W, W), lambda i, *_: (0, 0)),
            ],
            out_specs=pl.BlockSpec((FRONTS, ROWS, COLS, 24, BLK), lambda i, *_: (0, 0, 0, 0, 0)),
        ),
        out_shape=jax.ShapeDtypeStruct((FRONTS, ROWS, COLS, 24, BLK), jnp.float32),
    )(keep, info, local, parent)


def slice_kernel(inv_row_ref, inv_lead_ref, recv_ref, parent_ref, o_ref):
    for a in range(PR):
        for q in range(WB):
            total = parent_ref[a, :, q * BLK : (q + 1) * BLK]
            for front in range(FRONTS):
                r = inv_row_ref[front, a]
                c = inv_lead_ref[front, q]
                ok = jnp.logical_and(r >= 0, c >= 0).astype(jnp.float32)
                source = front * 32 + jnp.maximum(r, 0) * COLS + jnp.maximum(c, 0)
                total = total + recv_ref[source, 0:8] * ok
            o_ref[a, :, q * BLK : (q + 1) * BLK] = total


def assemble_slices(inv_row, inv_lead, recv, parent):
    smem = pl.BlockSpec(memory_space=pltpu.SMEM)
    vmem = pl.BlockSpec(memory_space=pltpu.VMEM)
    return pl.pallas_call(
        slice_kernel,
        name="slices",
        in_specs=[smem, smem, vmem, vmem],
        out_specs=vmem,
        out_shape=jax.ShapeDtypeStruct((PR, 8, W), jnp.float32),
    )(inv_row, inv_lead, recv, parent)


KB = 4


def factor_diagonal(get, put):
    groups = BLK // 8
    a = [get(g) for g in range(groups)]
    lanes = lax.broadcasted_iota(jnp.int32, (8, BLK), 1)
    subs = lax.broadcasted_iota(jnp.int32, (8, BLK), 0)
    e = [jnp.where(lanes == subs + 8 * g, 1.0, 0.0).astype(jnp.float32) for g in range(groups)]
    full = (8, BLK)
    for j0 in range(0, BLK, KB):
        g0, i0 = j0 // 8, j0 % 8
        head = [jnp.broadcast_to(a[g0][:, j0 + k : j0 + k + 1], full) for k in range(KB)]
        small = [[None] * KB for _ in range(KB)]
        for i in range(KB):
            for k in range(i + 1):
                small[i][k] = jnp.broadcast_to(head[k][i0 + i : i0 + i + 1, :], full)
        inv = [None] * KB
        low = [[None] * KB for _ in range(KB)]
        for k in range(KB):
            root = lax.rsqrt(small[k][k])
            inv[k] = root * (1.5 - 0.5 * small[k][k] * root * root)
            for i in range(k + 1, KB):
                low[i][k] = small[i][k] * inv[k]
            for i in range(k + 1, KB):
                for m in range(k + 1, i + 1):
                    small[i][m] = small[i][m] - low[i][k] * low[m][k]
        u, w = [], []
        for k in range(KB):
            r = jnp.broadcast_to(a[g0][i0 + k : i0 + k + 1, :], full)
            s = jnp.broadcast_to(e[g0][i0 + k : i0 + k + 1, :], full)
            for m in range(k):
                r = r - low[k][m] * u[m]
                s = s - low[k][m] * w[m]
            u.append(r * inv[k])
            w.append(s * inv[k])
        for g in range(g0, groups):
            if g == g0 and i0 + KB == 8:
                pass
            else:
                mult = []
                for k in range(KB):
                    c = head[k] if g == g0 else jnp.broadcast_to(a[g][:, j0 + k : j0 + k + 1], full)
                    for m in range(k):
                        c = c - mult[m] * low[k][m]
                    mult.append(c * inv[k])
                if g == g0:
                    mult = [jnp.where(subs >= i0 + KB, c, 0.0) for c in mult]
                for k in range(KB):
                    a[g] = a[g] - mult[k] * u[k]
                    e[g] = e[g] - mult[k] * w[k]
            if g == g0:
                for k in range(KB):
                    e[g] = jnp.where(subs == i0 + k, w[k], e[g])
        if i0 + KB == 8:
            put(g0, e[g0])


def factor_kernel(x_ref, high_ref, low_ref, m_ref, d_ref):
    for source in range(FRONTS * ROWS * COLS):
        row = source // COLS % ROWS
        group = source // 32 * COLS + source % COLS
        for j in range(2):
            p, q = (2 * row + j) // WB, (2 * row + j) % WB
            m_ref[p * BLK + group * 8 : p * BLK + group * 8 + 8, q * BLK : (q + 1) * BLK] = x_ref[
                source, 8 * j : 8 * j + 8
            ]
    lanes = lax.broadcasted_iota(jnp.int32, (BLK, BLK), 1)
    subs = lax.broadcasted_iota(jnp.int32, (BLK, BLK), 0)
    eye = jnp.where(lanes == subs, 1.0, 0.0).astype(jnp.float32)
    m_ref[:, W:] = jnp.zeros((W, W), jnp.float32)
    for block in range(W // BLK):
        m_ref[block * BLK : (block + 1) * BLK, W + block * BLK : W + (block + 1) * BLK] = eye

    def step(block, carry):
        base = pl.multiple_of(block * BLK, BLK)

        def get(g):
            return m_ref[pl.ds(pl.multiple_of(base + g * 8, 8), 8), pl.ds(base, BLK)]

        def put(g, value):
            d_ref[g * 8 : (g + 1) * 8, :] = value

        factor_diagonal(get, put)
        rows = jnp.dot(
            d_ref[...], m_ref[pl.ds(base, BLK), :], precision=HIGHEST, preferred_element_type=jnp.float32
        )
        m_ref[pl.ds(base, BLK), :] = rows

        @pl.when(block < W // BLK - 1)
        def _():
            column = lax.broadcasted_iota(jnp.int32, (BLK, W), 1)
            later = jnp.where(column >= base + BLK, rows[:, :W], 0.0)
            m_ref[...] = m_ref[...] - lax.dot_general(
                later, rows, (((0,), (0,)), ((), ())), precision=HIGHEST, preferred_element_type=jnp.float32
            )

        return carry

    lax.fori_loop(0, W // BLK, step, 0)
    inverse = m_ref[:, W:]
    high = inverse.astype(jnp.bfloat16)
    high_ref[...] = high
    low_ref[...] = (inverse - high.astype(jnp.float32)).astype(jnp.bfloat16)


def factor_inverse(tiles):
    vmem = pl.BlockSpec(memory_space=pltpu.VMEM)
    half = jax.ShapeDtypeStruct((W, W), jnp.bfloat16)
    return pl.pallas_call(
        factor_kernel,
        name="factor",
        in_specs=[vmem],
        out_specs=[vmem, vmem],
        out_shape=[half, half],
        scratch_shapes=[pltpu.VMEM((W, 2 * W), jnp.float32), pltpu.VMEM((BLK, BLK), jnp.float32)],
        compiler_params=pltpu.CompilerParams(vmem_limit_bytes=40 << 20),
    )(tiles)


def split(x):
    high = x.astype(jnp.bfloat16)
    return high, (x - high.astype(jnp.float32)).astype(jnp.bfloat16)


def three_products(x, high, low):
    def product(a, b):
        return lax.dot_general(a, b, (((1,), (1,)), ((), ())), preferred_element_type=jnp.float32)

    x_high, x_low = split(x)
    return (product(x_high, low) + product(x_low, high)) + product(x_high, high)


def panel_kernel(place_ref, *refs):
    rows, cols_ref = refs[:8], refs[8]
    inverse_high, inverse_low, panel_ref, high_ref, low_ref, block_ref = refs[9:]
    step = pl.program_id(0)

    def times_inverse(x):
        return three_products(x, inverse_high[...], inverse_low[...])

    @pl.when(step < PR)
    def _():
        for core in range(2):
            for col in range(COLS):
                for x in range(2):
                    source = place_ref[1] ^ (x * 8 + core * 4 + col)
                    start = pl.multiple_of(source * 8, 8)
                    block_ref[pl.ds(start, 8), :] = rows[core * COLS + col][x, 0]
        panel_ref[...] = times_inverse(block_ref[...])

    @pl.when(step >= PR)
    def _():
        value = times_inverse(cols_ref[:, 0].reshape(BLK, W))
        high_ref[...], low_ref[...] = split(value)


def make_panels(place, rows_raw, cols_raw, inverses):
    def in_rows(i):
        return jnp.minimum(i, PR - 1)

    def in_cols(i):
        return jnp.maximum(i - PR, 0)

    half = jax.ShapeDtypeStruct((PC * BLK, W), jnp.bfloat16)
    return pl.pallas_call(
        panel_kernel,
        name="panels",
        grid_spec=pltpu.PrefetchScalarGridSpec(
            num_scalar_prefetch=1,
            grid=(PR + PC,),
            in_specs=[pl.BlockSpec((2, 1, 8, W), lambda i, p: (0, in_rows(i), 0, 0))] * 8
            + [pl.BlockSpec((ROWS, 1, 16, W), lambda i, p: (0, in_cols(i), 0, 0))]
            + [pl.BlockSpec((W, W), lambda i, p: (0, 0))] * 2,
            out_specs=[
                pl.BlockSpec((BLK, W), lambda i, p: (in_rows(i), 0)),
                pl.BlockSpec((BLK, W), lambda i, p: (in_cols(i), 0)),
                pl.BlockSpec((BLK, W), lambda i, p: (in_cols(i), 0)),
            ],
            scratch_shapes=[pltpu.VMEM((BLK, W), jnp.float32)],
        ),
        out_shape=[jax.ShapeDtypeStruct((PR * BLK, W), jnp.float32), half, half],
        compiler_params=pltpu.CompilerParams(vmem_limit_bytes=32 << 20),
    )(place, *rows_raw, cols_raw, *inverses)


PAIR = 4


def final_kernel(inv_row_ref, inv_col_ref, lead_ref, *refs):
    recvs = refs[: PAIR * FRONTS]
    parent_ref, panel_ref, high_ref, low_ref = refs[PAIR * FRONTS : PAIR * FRONTS + 4]
    o_ref = refs[-1]
    step = pl.program_id(0)
    panel = panel_ref[:, 0].reshape(PAIR * HALF, W)
    product = three_products(panel, high_ref[...], low_ref[...])
    for part in range(PAIR):
        for b in range(PC):
            span = slice(b * BLK, (b + 1) * BLK)
            total = parent_ref[part, 0, :, span] - product[part * HALF : (part + 1) * HALF, span]
            for front in range(FRONTS):
                r = inv_row_ref[front, step * PAIR + part]
                c = inv_col_ref[front, b]
                ok = jnp.logical_and(r >= 0, c >= 0).astype(jnp.float32)
                total = total + recvs[part * FRONTS + front][jnp.maximum(c, 0)] * ok
            o_ref[part, 0, :, span] = total

    @pl.when(jnp.logical_and(lead_ref[0] == 1, step < WB // PAIR))
    def _():
        o_ref[...] = jnp.zeros_like(o_ref)

    @pl.when(lead_ref[1] == 1)
    def _():
        o_ref[:, :, :, :W] = jnp.zeros((PAIR, 1, HALF, W), jnp.float32)


def finish(place, inv_row, inv_col, lead, recv, parent, panel, high, low, before):
    def recv_map(part, front):
        return lambda i, ir, ic, ld: (
            front * ROWS + jnp.maximum(ir[front, i * PAIR + part], 0),
            0,
            0,
        )

    whole = pl.BlockSpec((PC * BLK, W), lambda a, *_: (0, 0))
    block = pl.BlockSpec((PAIR, 1, HALF, PC * BLK), lambda a, *_: (a, place, 0, 0))
    specs = [
        pl.BlockSpec((COLS, HALF, BLK), recv_map(part, front))
        for part in range(PAIR)
        for front in range(FRONTS)
    ]
    operands = [recv] * len(specs) + [
        parent.reshape(PR, 2, HALF, PC * BLK),
        panel.reshape(PR, 2, HALF, W),
        high,
        low,
    ]
    specs += [block, pl.BlockSpec((PAIR, 1, HALF, W), lambda a, *_: (a, place, 0, 0)), whole, whole]
    aliases = {}
    if before is not None:
        aliases = {3 + len(operands): 0}
        operands.append(before)
        specs.append(pl.BlockSpec(memory_space=pl.ANY))
    return pl.pallas_call(
        final_kernel,
        name="finish",
        grid_spec=pltpu.PrefetchScalarGridSpec(
            num_scalar_prefetch=3, grid=(PR // PAIR,), in_specs=specs, out_specs=block
        ),
        out_shape=jax.ShapeDtypeStruct((PR, 2, HALF, PC * BLK), jnp.float32),
        input_output_aliases=aliases,
        compiler_params=pltpu.CompilerParams(vmem_limit_bytes=56 << 20),
    )(inv_row, inv_col, lead, *operands)


def inverse_places(places, length):
    count = places.shape[1]
    hits = places[:, :, None] == jnp.arange(length, dtype=jnp.int32)
    order = jnp.arange(1, count + 1, dtype=jnp.int32)[None, :, None]
    return jnp.sum(jnp.where(hits, order, 0), axis=1) - 1


def flipped(x, axis, bits):
    size = lax.axis_size(axis)
    return lax.ppermute(x, axis, [(i, i ^ bits) for i in range(size)])


def swap_pairs(flip):
    pairs = []
    for front in range(FRONTS):
        for row in range(ROWS):
            for col in range(COLS):
                group = front * COLS + col
                half = group % 2 if flip == 0 else 1 - group % 2
                to_row, to_group = group // 2, 2 * row + half
                target = (to_group // COLS) * 32 + to_row * COLS + to_group % COLS
                pairs.append((front * 32 + row * COLS + col, target))
    return pairs


def body(parent_entries, child_update, child_map, child_mask):
    row = lax.axis_index("row")
    front = lax.axis_index("front")
    col = lax.axis_index("col")
    group = front * COLS + col
    local = child_update[0]
    window = lax.dynamic_slice(child_mask[0], (row * ROWS, col * GROUPS), (ROWS, GROUPS))

    lead_map = child_map.reshape(FRONTS, COLS, GROUPS)[:, :, 0]
    mine = lax.dynamic_index_in_dim(lead_map, front, 0, keepdims=False)
    p = lax.dynamic_index_in_dim(mine, row // 2, 0, keepdims=False)
    q = lax.dynamic_index_in_dim(mine, col, 0, keepdims=False)
    inside = (row % 2 == 0) & (p < WB) & (q < WB)
    corner_place = jnp.where(inside, p * WB + q, -1)
    holder = (row == 0) & (group == 0)
    info = jnp.stack([corner_place, holder.astype(jnp.int32)]).astype(jnp.int32)

    lead = make_lead(window[:, 0], info, local, parent_entries).reshape(128, 24, BLK)
    lead_recv = lax.all_to_all(lead, ALL, 0, 0, tiled=True)

    first = parent_entries[:, :W].reshape(PR, FRONTS, COLS, 8, W)
    sent = [lax.ppermute(first[:, :, k], "col", [(0, k)]) for k in range(1, COLS)]
    first = jnp.where(col == 0, first[:, :, 0], (sent[0] + sent[1]) + sent[2])

    tiles = jnp.sum(lead_recv[:, 8:], axis=0)
    tiles = jnp.broadcast_to(tiles[None], (128, 16, BLK))
    tiles = lax.all_to_all(tiles, ALL, 0, 0, tiled=True)

    upper, lower = pack(window, local)
    upper, first, tiles = lax.optimization_barrier((upper.reshape(128, HALF, BLK), first, tiles))
    upper_recv = lax.all_to_all(upper, ALL, 0, 0, tiled=True)
    inverses = factor_inverse(tiles)
    first, *inverses = lax.optimization_barrier((first, *inverses))

    sent = [lax.ppermute(first[:, k], "front", [(0, k)]) for k in range(1, FRONTS)]
    first = jnp.where(front == 0, first[:, 0], (sent[0] + sent[1]) + sent[2])

    column = group // 2 + 8 * (group % 2)
    by_row = lax.dynamic_index_in_dim(child_map.reshape(FRONTS, ROWS, 8), row, 2, keepdims=False)
    by_col = lax.dynamic_index_in_dim(
        child_map.reshape(FRONTS, COLS, GROUPS), column, 2, keepdims=False
    )
    inv_row = inverse_places(by_row - row * PR, PR)
    inv_col = inverse_places(by_col - group * PC, PC)
    inv_lead = inverse_places(lead_map, WB)

    slices = assemble_slices(inv_row, inv_lead, lead_recv, first)

    place = jnp.stack([row, group]).astype(jnp.int32)

    even = group % 2 == 0
    one = lax.ppermute(jnp.where(even, slices[:PC], slices[PC:]), ALL, swap_pairs(0))
    two = lax.ppermute(jnp.where(even, slices[PC:], slices[:PC]), ALL, swap_pairs(1))
    mine = jnp.stack([jnp.where(even, one, two), jnp.where(even, two, one)], axis=1)
    mine = mine.reshape(PC, 16, W)
    pair = jnp.stack([slices, flipped(slices, "front", 2)])
    pair, mine = lax.optimization_barrier((pair, mine))
    pair = [pair] + [flipped(pair, "col", bits) for bits in range(1, COLS)]
    rows_raw = pair + [flipped(x, "front", 1) for x in pair]

    mine, upper_recv = lax.optimization_barrier((mine, upper_recv))
    mine = jnp.broadcast_to(mine.reshape(1, PC * 16, W), (ROWS, PC * 16, W))
    cols_raw = lax.all_to_all(mine, "row", 0, 0, tiled=True).reshape(ROWS, PC, 16, W)

    lower, cols_raw, rows_raw = lax.optimization_barrier(
        (lower.reshape(128, HALF, BLK), cols_raw, rows_raw)
    )
    lower_recv = lax.all_to_all(lower, ALL, 0, 0, tiled=True)
    panel, high, low = make_panels(place, rows_raw, cols_raw, inverses)
    lead_flags = jnp.stack([row == 0, group == 0]).astype(jnp.int32)
    args = (parent_entries, panel, high, low)
    schur = finish(0, inv_row, inv_col, lead_flags, upper_recv, *args, None)
    schur = finish(1, inv_row, inv_col, lead_flags, lower_recv, *args, schur)
    return schur.reshape(PR * BLK, PC * BLK), panel


def solution(mesh):
    placed = (P("row", ("front", "col")), P("front", "row", "col"), P(), P("front", None, None))
    return jax.shard_map(
        body,
        mesh=mesh,
        in_specs=placed,
        out_specs=(P("row", ("front", "col")), P("row", None)),
        check_vma=False,
    )
```
